32 devices in a mesh: expert: 16 (over z, y, x), tensor: 2 (over core).
Axes of the slice: x: 2, y: 2, z: 4, core: 2. Of those that a mesh axis runs over, the one named last changes fastest.
Arguments:
- hidden_in: bfloat16 [16384, 768], P('expert'), may hold values from -6 to 6
- w_qkv: bfloat16 [768, 3, 768], P(None, None, 'tensor'), may hold values from -0.21875 to 0.21875
- w_out: bfloat16 [768, 768], P('tensor'), may hold values from -0.875 to 0.875
- gain_in: float32 [768], replicated, may hold values from 0.5 to 1.5
- gain_mid: float32 [768], replicated, may hold values from 0.5 to 1.5
- w_router: bfloat16 [768, 12], replicated, may hold values from -0.109375 to 0.109375
- w_const: bfloat16 [768, 4], replicated, may hold values from -0.21875 to 0.21875
- const_vec: float32 [2, 768], replicated, may hold values from -5 to 5
- w_gate: bfloat16 [8, 768, 2048], P(None, 'expert', 'tensor'), may hold values from -0.21875 to 0.21875
- w_up: bfloat16 [8, 768, 2048], P(None, 'expert', 'tensor'), may hold values from -0.21875 to 0.21875
- w_down: bfloat16 [8, 768, 2048], P(None, 'expert', 'tensor'), may hold values from -0.125 to 0.125
- prev_logits: float32 [16384, 12], P('expert'), may hold values from -3 to 3
- routes: int32 [16384, 2], P('expert'), may hold values from 0 to 11, all different within a row
- doc_ids: int32 [16384], P('expert'), may hold values from 0 to 3, as said below
- span_start: int32 [16, 2], P('expert'), may hold values from 0 to 768, as said below
- span_len: int32 [16, 2], P('expert'), may hold values from 64 to 256, as said below
- d_output: bfloat16 [16384, 768], P('expert'), may hold values from -6 to 6
Outputs:
- output: bfloat16 [16384, 768], P('expert')
- grad_input: bfloat16 [16384, 768], P('expert')
- grad_prev: float32 [16384, 12], P('expert')
- grad_qkv: float32 [768, 3, 768], P('expert', None, 'tensor')
- grad_wout: float32 [768, 768], P('tensor', 'expert')
- grad_gain_in: float32 [768], P('expert')
- grad_gain_mid: float32 [768], P('expert')
- grad_router: float32 [768, 12], P('expert')
- grad_const: float32 [768, 4], P('expert')
- grad_cvec: float32 [2, 768], P(None, 'expert')
- grad_gate: float32 [8, 768, 2048], P(None, 'expert', 'tensor')
- grad_up: float32 [8, 768, 2048], P(None, 'expert', 'tensor')
- grad_down: float32 [8, 768, 2048], P(None, 'expert', 'tensor')
The draws below stay inside these ranges and needn't reach their ends.
Inputs may be any that keep to these rules, and one draw needn't show every extreme that they name: routes below 8 name feed-forward experts; 8 is the zero expert, 9 the copy expert, 10 and 11 the constant experts. `doc_ids`: within each sequence ids never fall and split it into up to four documents; some sequence is a single document. `span_start`: span j of a sequence lies inside the j-th of 2 equal parts of it. `span_len`: some span of every sequence has exactly 256 tokens.
All inputs are finite; a program needn't handle non-finite values.
Results may differ from the reference program's by a relative error of at most 0.017.
Values may be sent and summed in bfloat16 or wider, within the bound.
No kernel may reach another device: no remote copies, remote signals or barrier semaphores. Data moves between devices by JAX's collectives and lax.ppermute only.
A program may use at most 192 MiB of HBM per device.

```python
import jax
import jax.numpy as jnp
from jax import lax

D = 768
HEADS = 12
HD = 64
FF = 2048
EXPERTS = 8
TOK_DEV = 1024
NSPAN = 2
SPAN_MAX = 256
SEQS = 16
TOKENS = 16384
NR = 12
CAP = 176
HHD = 768


def span_table(key):
    key_len, key_off, key_top, key_first, key_last = jax.random.split(key, 5)
    lengths = jax.random.randint(key_len, (SEQS, NSPAN), SPAN_MAX // 4, SPAN_MAX + 1)
    longest = jax.random.randint(key_top, (SEQS,), 0, NSPAN)
    lengths = jnp.where(jnp.arange(NSPAN)[None, :] == longest[:, None], SPAN_MAX, lengths)
    region = TOK_DEV // NSPAN
    offsets = jax.random.randint(key_off, (SEQS, NSPAN), 0, region - SPAN_MAX + 1)
    first_seq = jax.random.randint(key_first, (), 0, SEQS)
    last_seq = jax.random.randint(key_last, (), 0, SEQS)
    seq_ids = jnp.arange(SEQS)[:, None]
    span_ids = jnp.arange(NSPAN)[None, :]
    offsets = jnp.where((seq_ids == first_seq) & (span_ids == 0), 0, offsets)
    offsets = jnp.where((seq_ids == last_seq) & (span_ids == NSPAN - 1), region - SPAN_MAX, offsets)
    starts = span_ids * region + offsets
    return (starts.astype(jnp.int32), lengths.astype(jnp.int32))


def draw_span_start(key, part):
    return span_table(jax.random.fold_in(key, 11))[0]


def draw_span_len(key, part):
    return span_table(jax.random.fold_in(key, 11))[1]


def draw_doc_ids(key, part):
    key_cut, key_whole, key_pick = jax.random.split(jax.random.fold_in(key, 23), 3)
    cuts = jax.random.randint(key_cut, (SEQS, 3), 1, TOK_DEV)
    single = (jax.random.randint(key_whole, (SEQS,), 0, 4) == 0) | (jnp.arange(SEQS) == jax.random.randint(key_pick, (), 0, SEQS))
    cuts = jnp.where(single[:, None], TOK_DEV, cuts)
    position = jnp.arange(TOK_DEV)
    ids_table = jnp.sum((position[None, :, None] >= cuts[:, None, :]).astype(jnp.int32), axis=2)
    return ids_table.reshape(SEQS * TOK_DEV).astype(jnp.int32)


def level_of(own_key, shape, pieces, least, largest):
    factor_of = 1.0
    for axis_at, shards_of in pieces:
        heights = jax.random.uniform(jax.random.fold_in(jax.random.fold_in(own_key, 6), axis_at), (shards_of,), jnp.float32, least / len(pieces), largest / len(pieces))
        factor_of = factor_of * jnp.repeat(jnp.exp(heights), shape[axis_at] // shards_of).reshape((-1,) + (1,) * (len(shape) - 1 - axis_at))
    return factor_of


def different_ones(key, rows, count, top, lift):
    order = jax.random.permutation(jax.random.fold_in(key, 1), count)
    favour = order
    for power in range(3):
        favour = favour * favour // count
    favour = favour * lift // count
    tickets = jax.random.randint(jax.random.fold_in(key, 2), (rows, count), 0, 4096) + favour
    holders = jax.random.permutation(jax.random.fold_in(key, 3), rows)[jnp.arange(count) % rows]
    tickets = jnp.where(jnp.arange(rows)[:, None] == holders[None, :], 1 << 14, tickets)
    merit = tickets * count + jnp.arange(count)
    return lax.top_k(merit.astype(jnp.int32), top)[1].astype(jnp.int32)


def bell_draw(key, extent, scale, most, shards=(), kind=jnp.bfloat16):
    values = scale * jax.random.normal(key, extent, jnp.float32)
    if shards:
        values = values * level_of(key, extent, shards, -0.22, 0.18)
    return jnp.clip(values, -most, most).astype(kind)


def setup_inputs(seed: int = 0) -> dict:
    key_list = jax.random.split(jax.random.key(seed), 18)
    return {
        "hidden_in": bell_draw(key_list[0], (TOKENS, D), 1.0, 6.0, ((0, 16),)),
        "w_qkv": bell_draw(key_list[1], (D, 3, HHD), D ** -0.5, 0.21875, ((2, 2),)),
        "w_out": bell_draw(key_list[2], (HHD, D), (HHD // 16) ** -0.5, 0.875, ((0, 2),)),
        "gain_in": jnp.clip(1.0 + 0.1 * jax.random.normal(key_list[3], (D,), jnp.float32), 0.5, 1.5),
        "gain_mid": jnp.clip(1.0 + 0.1 * jax.random.normal(key_list[4], (D,), jnp.float32), 0.5, 1.5),
        "w_router": bell_draw(key_list[5], (D, NR), (4 * D) ** -0.5, 0.109375),
        "w_const": bell_draw(key_list[6], (D, 4), D ** -0.5, 0.21875),
        "const_vec": bell_draw(key_list[7], (2, D), 1.0, 5.0, (), jnp.float32),
        "w_gate": bell_draw(key_list[8], (EXPERTS, D, FF), D ** -0.5, 0.21875, ((1, 16), (2, 2))),
        "w_up": bell_draw(key_list[9], (EXPERTS, D, FF), D ** -0.5, 0.21875, ((1, 16), (2, 2))),
        "w_down": bell_draw(key_list[10], (EXPERTS, D, FF), FF ** -0.5, 0.125, ((1, 16), (2, 2))),
        "prev_logits": bell_draw(key_list[11], (TOKENS, NR), 0.5, 3.0, ((0, 16),), jnp.float32),
        "routes": different_ones(key_list[12], TOKENS, NR, 2, 1365),
        "doc_ids": draw_doc_ids(jax.random.fold_in(key_list[17], 71), 0),
        "span_start": draw_span_start(jax.random.fold_in(key_list[17], 71), 0),
        "span_len": draw_span_len(jax.random.fold_in(key_list[17], 71), 0),
        "d_output": bell_draw(key_list[16], (TOKENS, D), 1.0, 6.0, ((0, 16),)),
    }


EPSILON = 1e-06
PRECISE = lax.Precision.HIGHEST

@jax.custom_vjp
def low(v):
    return lax.optimization_barrier(v.astype(jnp.bfloat16)).astype(jnp.float32)

@jax.custom_vjp
def low_back(v):
    return v

def low_keep(v):
    return (low(v), None)

def low_pass(kept, grad):
    return (grad,)

def back_keep(v):
    return (v, None)

def back_low(kept, grad):
    return (low(grad),)
low.defvjp(low_keep, low_pass)
low_back.defvjp(back_keep, back_low)

def rms_norm(values, gain_vec):
    return values * lax.rsqrt(lax.optimization_barrier(jnp.mean(values * values, axis=-1, keepdims=True)) + EPSILON) * gain_vec

def angles(length):
    half_dim = HD // 2
    position = jnp.arange(length).astype(jnp.float32)
    frequency = 10000.0 ** (-jnp.arange(half_dim).astype(jnp.float32) / half_dim)
    phase_tab = position[:, None] * frequency[None, :]
    return (jnp.cos(phase_tab)[:, None, :], jnp.sin(phase_tab)[:, None, :])

def rotate(values, cosine, sine_tab):
    half_dim = values.shape[-1] // 2
    first_half = values[..., :half_dim]
    second_half = values[..., half_dim:]
    return jnp.concatenate([first_half * cosine - second_half * sine_tab, second_half * cosine + first_half * sine_tab], axis=-1)

def span_index(starts, lengths):
    position = jnp.arange(TOK_DEV)[:, None]
    inside = (position >= starts[None, :]) & (position < starts[None, :] + lengths[None, :])
    return lax.optimization_barrier(jnp.sum(jnp.where(inside, jnp.arange(1, NSPAN + 1)[None, :], 0), axis=1))

def visible_mask(documents, span_of):
    position = jnp.arange(TOK_DEV)
    same_doc = documents[:, None] == documents[None, :]
    causal = position[None, :] <= position[:, None]
    same_span = (span_of[:, None] == span_of[None, :]) & (span_of[:, None] > 0)
    return same_doc & (causal | same_span)

def attend_sequence(normed_seq, qkv_mat, documents, span_of, cosine, sine_tab):
    projected = low_back(jnp.einsum('td,dce->tce', normed_seq, qkv_mat, precision=PRECISE))
    head_shape = (TOK_DEV, HEADS, HD)
    queries = low(rotate(projected[:, 0].reshape(head_shape), cosine, sine_tab))
    keys_rot = low(rotate(projected[:, 1].reshape(head_shape), cosine, sine_tab))
    value_rows = low(projected[:, 2].reshape(head_shape))
    scores = low_back(jnp.einsum('qhe,khe->hqk', queries, keys_rot, precision=PRECISE) * HD ** (-0.5))
    scores = jnp.where(visible_mask(documents, span_of)[None], scores, -1e+30)
    row_max = lax.optimization_barrier(jnp.max(scores, axis=-1, keepdims=True))
    weights = jnp.exp(scores - row_max)
    soft_probs = low(weights / lax.optimization_barrier(jnp.sum(weights, axis=-1, keepdims=True)))
    context = jnp.einsum('hqk,khe->qhe', soft_probs, value_rows, precision=PRECISE).reshape(TOK_DEV, HHD)
    return low_back(low(context))

def expert_ffn(padded, slot_tok, gate_mat, up_mat, down_mat):
    slot_rows = low_back(padded[slot_tok])
    gate_pre = low_back(jnp.dot(slot_rows, gate_mat, precision=PRECISE))
    up_pre = low_back(jnp.dot(slot_rows, up_mat, precision=PRECISE))
    hidden = low(jax.nn.silu(gate_pre) * up_pre)
    return low_back(low(jnp.einsum('cf,df->cd', hidden, down_mat, precision=PRECISE)))

def reference(hidden_in, w_qkv, w_out, gain_in, gain_mid, w_router, w_const, const_vec, w_gate, w_up, w_down, prev_logits, routes, doc_ids, span_start, span_len, d_output):
    pair_routes = routes.reshape(SEQS, 2 * TOK_DEV)
    route_hot = (pair_routes[:, :, None] == jnp.arange(NR)[None, None, :]).astype(jnp.int32)
    earlier = jnp.cumsum(route_hot, axis=1) - route_hot
    position = lax.optimization_barrier(jnp.sum(earlier * route_hot, axis=-1))
    kept_pair = (pair_routes < EXPERTS) & (position < CAP)
    source = jnp.arange(SEQS)[:, None]
    dummy_slot = EXPERTS * SEQS * CAP
    slot_of = jnp.where(kept_pair, pair_routes * (SEQS * CAP) + source * CAP + position, dummy_slot).reshape(TOKENS * 2).astype(jnp.int32)
    token_of = (source * TOK_DEV + jnp.arange(2 * TOK_DEV)[None, :] // 2).reshape(TOKENS * 2).astype(jnp.int32)
    slot_tok = jnp.full((dummy_slot + 1,), TOKENS, jnp.int32).at[slot_of].set(token_of)[:dummy_slot].reshape(EXPERTS, SEQS * CAP)
    span_of = jax.vmap(span_index)(span_start, span_len)
    documents = doc_ids.reshape(SEQS, TOK_DEV)
    cosine, sine_tab = angles(TOK_DEV)
    group_size = max(1, min(SEQS, 4096 // TOK_DEV))
    attend_group = jax.checkpoint(jax.vmap(attend_sequence, in_axes=(0, None, 0, 0, None, None)))
    ffn_step = jax.checkpoint(expert_ffn)

    def forward(hidden_f, qkv_f, wout_f, gain_in_f, gain_mid_f, router_f, const_f, cvec_f, gate_f, up_f, down_f, prev_f):
        normed_in = low(rms_norm(hidden_f, gain_in_f))
        grouped = (normed_in.reshape(SEQS // group_size, group_size, TOK_DEV, D), documents.reshape(SEQS // group_size, group_size, TOK_DEV), span_of.reshape(SEQS // group_size, group_size, TOK_DEV))
        context = lax.map(lambda operands: attend_group(operands[0], qkv_f, operands[1], operands[2], cosine, sine_tab), grouped).reshape(TOKENS, HHD)
        attended = low_back(jnp.dot(context, wout_f, precision=PRECISE))
        residual_mid = hidden_f + attended
        normed_f = rms_norm(residual_mid, gain_mid_f)
        normed_mid = low(normed_f)
        logits = low_back(jnp.dot(normed_mid, router_f, precision=PRECISE)) + prev_f
        const_logits = low_back(jnp.dot(normed_mid, const_f, precision=PRECISE))
        gate_probs = jax.nn.softmax(jnp.take_along_axis(logits, routes, axis=1), axis=1)
        padded = jnp.concatenate([normed_mid, jnp.zeros((1, D), normed_mid.dtype)], axis=0)
        expert_out = lax.map(lambda operands: ffn_step(padded, operands[0], operands[1], operands[2], operands[3]), (slot_tok, gate_f, up_f, down_f))
        padded_out = jnp.concatenate([expert_out.reshape(EXPERTS * SEQS * CAP, D), jnp.zeros((1, D), expert_out.dtype)], axis=0)
        pair_out = padded_out[slot_of].reshape(TOKENS, 2, D)
        mixing = jax.nn.softmax(const_logits.reshape(TOKENS, 2, 2), axis=-1)
        const_out = mixing[:, :, 0:1] * normed_f[:, None, :] + mixing[:, :, 1:2] * cvec_f[None, :, :]
        route_col = routes[:, :, None]
        pair_out = pair_out + jnp.where(route_col == EXPERTS + 1, normed_f[:, None, :], 0.0)
        pair_out = pair_out + jnp.where(route_col == EXPERTS + 2, const_out[:, 0:1, :], 0.0)
        pair_out = pair_out + jnp.where(route_col == EXPERTS + 3, const_out[:, 1:2, :], 0.0)
        return residual_mid + lax.optimization_barrier(jnp.sum(gate_probs[:, :, None] * pair_out, axis=1))
    primals = tuple((array_in.astype(jnp.float32) for array_in in (hidden_in, w_qkv, w_out, gain_in, gain_mid, w_router, w_const, const_vec, w_gate, w_up, w_down, prev_logits)))
    output, pullback = jax.vjp(forward, *primals)
    gradients = pullback(d_output.astype(jnp.float32))
    return (output.astype(jnp.bfloat16), gradients[0].astype(jnp.bfloat16), gradients[11], gradients[1], gradients[2], gradients[3], gradients[4], gradients[5], gradients[6], gradients[7], gradients[8], gradients[9], gradients[10])
```

```python
import functools

import jax
import jax.numpy as jnp
import numpy as np
from jax import lax
from jax.experimental import pallas as pl
from jax.experimental.pallas import tpu as pltpu
from jax.sharding import PartitionSpec as P

HD = 64
CAP = 176
PARTS = 2
EPSILON = 1e-06
BF = jnp.bfloat16
F32 = jnp.float32
NEG = -1e30
VMEM_LIMIT = 56 * 1024 * 1024


def nn(a, b):
    return lax.dot_general(a, b, (((1,), (0,)), ((), ())), preferred_element_type=F32)


def nt(a, b):
    return lax.dot_general(a, b, (((1,), (1,)), ((), ())), preferred_element_type=F32)


def tn(a, b):
    return lax.dot_general(a, b, (((0,), (0,)), ((), ())), preferred_element_type=F32)


def iota(shape, dim):
    return lax.broadcasted_iota(jnp.int32, shape, dim)


def params(**kw):
    return pltpu.CompilerParams(vmem_limit_bytes=VMEM_LIMIT, **kw)


def cost(flops, nbytes, trans=0):
    return pl.CostEstimate(flops=int(flops), bytes_accessed=int(nbytes), transcendentals=int(trans))


def whole(shape):
    return pl.BlockSpec(shape, lambda *_: (0,) * len(shape))


SMEM = pl.BlockSpec(memory_space=pltpu.SMEM)


def swap_halves(values):
    width = values.shape[1]
    half = HD // 2
    lane = iota(values.shape, 1)
    ahead = pltpu.roll(values, width - half, 1)
    behind = pltpu.roll(values, half, 1)
    return jnp.where(lax.rem(lane, HD) < half, ahead, behind)


def qkv_body(h_ref, gain_ref, w_ref, cos_ref, sin_ref, n_ref, q_ref, k_ref, v_ref):
    h = h_ref[...].astype(F32)
    inv = lax.rsqrt(jnp.mean(h * h, axis=-1, keepdims=True) + EPSILON)
    normed = (h * inv * gain_ref[...]).astype(BF)
    n_ref[...] = normed
    copies = q_ref.shape[1] // 128
    cos = jnp.concatenate([cos_ref[...]] * copies, axis=1)
    sin = jnp.concatenate([sin_ref[...]] * copies, axis=1)
    q = nn(normed, w_ref[0])
    q_ref[...] = ((q * cos + swap_halves(q) * sin) * (HD**-0.5)).astype(BF)
    k = nn(normed, w_ref[1])
    k_ref[...] = (k * cos + swap_halves(k) * sin).astype(BF)
    v_ref[...] = nn(normed, w_ref[2]).astype(BF)


def qkv(hidden, gain, w3, cos, sin):
    length, width = hidden.shape
    inner = w3.shape[2]
    blk = 256
    row = lambda n: pl.BlockSpec((blk, n), lambda i: (i, 0))
    return pl.pallas_call(
        qkv_body,
        grid=(length // blk,),
        in_specs=[row(width), whole((1, width)), whole(w3.shape), row(128), row(128)],
        out_specs=[row(width), row(inner), row(inner), row(inner)],
        out_shape=[jax.ShapeDtypeStruct((length, width), BF)]
        + [jax.ShapeDtypeStruct((length, inner), BF)] * 3,
        compiler_params=params(),
        cost_estimate=cost(2 * length * width * inner * 3, 10 << 20),
        name="qkv",
    )(hidden, gain, w3, cos, sin)


def document_of(position, meta_ref):
    doc = jnp.zeros(position.shape, jnp.int32)
    for j in range(3):
        doc = doc + (position >= meta_ref[4 + j]).astype(jnp.int32)
    return doc


def span_of(position, meta_ref):
    span = jnp.zeros(position.shape, jnp.int32)
    for j in range(PARTS):
        inside = (position >= meta_ref[j]) & (position < meta_ref[2 + j])
        span = jnp.where(inside, span + (j + 1), span)
    return span


def mask_bias(query_pos, key_pos, meta_ref):
    query_span = span_of(query_pos, meta_ref)
    query_span = jnp.where(query_span == 0, -1, query_span)
    key_span = span_of(key_pos, meta_ref)
    same_doc = document_of(query_pos, meta_ref) == document_of(key_pos, meta_ref)
    seen = same_doc & ((key_pos <= query_pos) | (query_span == key_span))
    return jnp.where(seen, 0.0, NEG)


def attend_body(meta_ref, q_ref, k_ref, v_ref, ctx_ref, lse_ref, bias_ref):
    block = pl.program_id(0)
    pair = pl.program_id(1)
    rows, total = bias_ref.shape
    chunk = 256

    def run(keys):
        @pl.when(pair == 0)
        def _():
            for c in range(rows // chunk):
                qpos = block * rows + c * chunk + iota((chunk, 1), 0)
                kpos = iota((1, keys), 1)
                bias_ref[c * chunk : (c + 1) * chunk, :keys] = mask_bias(qpos, kpos, meta_ref)

        lane = iota((1, 128), 1)

        def step(c, carry):
            at = pl.multiple_of(c * chunk, chunk)
            q = q_ref[pl.ds(at, chunk), :]
            bias = bias_ref[pl.ds(at, chunk), :keys]
            k = k_ref[:keys, :]
            v = v_ref[:keys, :]
            outs = []
            for head in range(2):
                own = (lane // HD) == head
                qh = jnp.where(own, q, jnp.zeros_like(q))
                s = nt(qh, k) + bias
                top = jnp.max(s, axis=-1, keepdims=True)
                p = jnp.exp(s - top).astype(BF)
                mixed = nn(p, jnp.where(own, v, jnp.ones_like(v)))
                norm = pltpu.roll(mixed, HD, 1)
                outs.append((mixed / norm, top + jnp.log(norm)))
            first = lane < HD
            ctx_ref[pl.ds(at, chunk), :] = jnp.where(first, outs[0][0], outs[1][0]).astype(BF)
            lse = jnp.where(first, outs[0][1], outs[1][1]).T
            at2 = pl.multiple_of(block * rows + c * chunk, chunk)
            lse_ref[pl.ds(2 * pair, 1), pl.ds(at2, chunk)] = lse[0:1]
            lse_ref[pl.ds(2 * pair + 1, 1), pl.ds(at2, chunk)] = lse[HD : HD + 1]
            return carry

        lax.fori_loop(0, rows // chunk, step, 0)

    for b in range(PARTS):

        @pl.when(block == b)
        def _(b=b):
            run((b + 1) * rows)


def attend(meta, q, k, v):
    length, inner = q.shape
    pairs = inner // 128
    rows = length // PARTS
    heads8 = 8 * ((2 * pairs + 7) // 8)
    return pl.pallas_call(
        attend_body,
        grid=(PARTS, pairs),
        in_specs=[
            SMEM,
            pl.BlockSpec((rows, 128), lambda b, p: (b, p)),
            pl.BlockSpec((length, 128), lambda b, p: (0, p)),
            pl.BlockSpec((length, 128), lambda b, p: (0, p)),
        ],
        out_specs=[
            pl.BlockSpec((rows, 128), lambda b, p: (b, p)),
            whole((heads8, length)),
        ],
        out_shape=[
            jax.ShapeDtypeStruct((length, inner), BF),
            jax.ShapeDtypeStruct((heads8, length), F32),
        ],
        scratch_shapes=[pltpu.VMEM((rows, length), F32)],
        compiler_params=params(),
        cost_estimate=cost(4 * length * length * inner, 8 << 20, length * length * 6),
        name="attend",
    )(meta, q, k, v)


def attend_back_body(
    meta_ref, q_ref, k_ref, v_ref, ctx_ref, lse_ref, ag_ref, wo_ref, cos_ref, sin_ref,
    pq_ref, pk_ref, pv_ref, bias_ref, do_ref, delta_ref, dq0_ref, dq1_ref, sl_ref,
):
    pair = pl.program_id(0)
    length = q_ref.shape[0]
    rows = length // PARTS
    chunk = 256
    lane = iota((1, 128), 1)
    first = lane < HD

    @pl.when(pair == 0)
    def _():
        def fill(c, carry):
            at = pl.multiple_of(c * chunk, chunk)
            kpos = at + iota((chunk, 1), 0)
            qpos = iota((1, length), 1)
            bias_ref[pl.ds(at, chunk), :] = mask_bias(qpos, kpos, meta_ref)
            return carry

        lax.fori_loop(0, length // chunk, fill, 0)

    def prepare(c, carry):
        at = pl.multiple_of(c * chunk, chunk)
        grad = nt(ag_ref[pl.ds(at, chunk), :], wo_ref[...]).astype(BF)
        do_ref[pl.ds(at, chunk), :] = grad
        prod = (grad.astype(F32) * ctx_ref[pl.ds(at, chunk), :].astype(F32)).T
        delta_ref[0:1, pl.ds(at, chunk)] = jnp.sum(prod[:HD], axis=0, keepdims=True)
        delta_ref[1:2, pl.ds(at, chunk)] = jnp.sum(prod[HD:], axis=0, keepdims=True)
        return carry

    lax.fori_loop(0, length // chunk, prepare, 0)
    dq0_ref[...] = jnp.zeros_like(dq0_ref)
    dq1_ref[...] = jnp.zeros_like(dq1_ref)

    def step(c, carry, start):
        count = length - start
        at = pl.multiple_of(c * chunk, chunk)
        k = k_ref[pl.ds(at, chunk), :]
        v = v_ref[pl.ds(at, chunk), :]
        bias = bias_ref[pl.ds(at, chunk), start:]
        q = q_ref[start:, :]
        grad = do_ref[start:, :]
        dks = []
        dvs = []
        for head in range(2):
            own = (lane // HD) == head
            kh = jnp.where(own, k, jnp.zeros_like(k))
            vh = jnp.where(own, v, jnp.zeros_like(v))
            lse = lse_ref[pl.ds(2 * pair + head, 1), start:]
            p = jnp.exp(nt(kh, q) + bias - lse)
            dvs.append(nn(p.astype(BF), grad))
            dp = nt(vh, grad)
            ds = (p * (dp - delta_ref[head : head + 1, start:])).astype(BF)
            dks.append(nn(ds, q))
            dq_ref = dq0_ref if head == 0 else dq1_ref
            dq_ref[start:, :] += tn(ds, k)
        dk = jnp.where(first, dks[0], dks[1])
        cos = cos_ref[pl.ds(at, chunk), :]
        sin = sin_ref[pl.ds(at, chunk), :]
        pk_ref[pl.ds(at, chunk), :] = (dk * cos - swap_halves(dk) * sin).astype(BF)
        pv_ref[pl.ds(at, chunk), :] = jnp.where(first, dvs[0], dvs[1]).astype(BF)
        return carry

    for b in range(PARTS):
        per = rows // chunk
        lax.fori_loop(b * per, (b + 1) * per, functools.partial(step, start=b * rows), 0)

    def finish(c, carry):
        at = pl.multiple_of(c * chunk, chunk)
        dq = jnp.where(first, dq0_ref[pl.ds(at, chunk), :], dq1_ref[pl.ds(at, chunk), :])
        dq = dq * (HD**-0.5)
        cos = cos_ref[pl.ds(at, chunk), :]
        sin = sin_ref[pl.ds(at, chunk), :]
        pq_ref[pl.ds(at, chunk), :] = (dq * cos - swap_halves(dq) * sin).astype(BF)
        return carry

    lax.fori_loop(0, length // chunk, finish, 0)


def attend_back(meta, q, k, v, ctx, lse, agrad, w_out, cos, sin):
    length, inner = q.shape
    width = agrad.shape[1]
    pairs = inner // 128
    col = pl.BlockSpec((length, 128), lambda p: (0, p))
    return pl.pallas_call(
        attend_back_body,
        grid=(pairs,),
        in_specs=[
            SMEM, col, col, col, col, whole(lse.shape), whole((length, width)),
            pl.BlockSpec((128, width), lambda p: (p, 0)),
            whole((length, 128)), whole((length, 128)),
        ],
        out_specs=[col, col, col],
        out_shape=[jax.ShapeDtypeStruct((length, inner), BF)] * 3,
        scratch_shapes=[
            pltpu.VMEM((length, length), F32),
            pltpu.VMEM((length, 128), BF),
            pltpu.VMEM((8, length), F32),
            pltpu.VMEM((length, 128), F32),
            pltpu.VMEM((length, 128), F32),
            pltpu.VMEM((8, 128), F32),
        ],
        compiler_params=params(),
        cost_estimate=cost(10 * length * length * inner, 12 << 20, length * length * 6),
        name="attend_back",
    )(meta, q, k, v, ctx, lse, agrad, w_out, cos, sin)


def mid_body(
    tid_ref, h_ref, a_ref, b_ref, gain_ref, joint_ref, prev_ref, routes_ref, og_ref,
    r_ref, n_ref, send_ref, rows_ref, cols_ref, lg_ref, col_ref,
):
    length = h_ref.shape[0]
    width = h_ref.shape[1]
    routes_total = prev_ref.shape[0]
    experts = routes_total - 4
    half = CAP // 2
    slots = send_ref.shape[0]
    chunk = 256
    tid = tid_ref[0]

    def norm(c, carry):
        at = pl.multiple_of(c * chunk, chunk)
        r = h_ref[pl.ds(at, chunk), :].astype(F32) + (
            a_ref[pl.ds(at, chunk), :] + b_ref[pl.ds(at, chunk), :]
        )
        r_ref[pl.ds(at, chunk), :] = r
        inv = lax.rsqrt(jnp.mean(r * r, axis=-1, keepdims=True) + EPSILON)
        normed = (r * inv * gain_ref[...]).astype(BF)
        n_ref[pl.ds(at, chunk), :] = normed
        lg_ref[:, pl.ds(at, chunk)] = nt(joint_ref[...], normed)
        return carry

    lax.fori_loop(0, length // chunk, norm, 0)

    lg = lg_ref[...]
    logits = lg[:routes_total] + prev_ref[...]
    route = [routes_ref[k : k + 1, :] for k in range(2)]
    rid = iota((routes_total, length), 0)
    chosen = [jnp.sum(jnp.where(rid == r, logits, 0.0), axis=0, keepdims=True) for r in route]
    top = jnp.maximum(chosen[0], chosen[1])
    raised = [jnp.exp(c - top) for c in chosen]
    total = raised[0] + raised[1]
    gate = [e / total for e in raised]

    rid16 = iota((16, length), 0)
    hot = ((rid16 == route[0]) | (rid16 == route[1])).astype(F32)
    blk = 256
    upper = (iota((blk, blk), 0) < iota((blk, blk), 1)).astype(BF)
    before = jnp.zeros((16, 1), F32)
    parts = []
    for c in range(length // blk):
        part = hot[:, c * blk : (c + 1) * blk]
        parts.append(nn(part.astype(BF), upper) + before)
        before = before + jnp.sum(part, axis=1, keepdims=True)
    count = jnp.concatenate(parts, axis=1)
    column = []
    for k in range(2):
        pos = jnp.sum(jnp.where(rid16 == route[k], count, 0.0), axis=0, keepdims=True)
        pos = pos.astype(jnp.int32)
        kept = (route[k] < experts) & (pos < CAP)
        side = (pos >= half).astype(jnp.int32)
        col = jnp.where(side == tid, 0, slots) + route[k] * half + pos - side * half
        column.append(jnp.where(kept, col, -1))
    mix = []
    for j in range(2):
        c0 = lg[routes_total + 2 * j : routes_total + 2 * j + 1]
        c1 = lg[routes_total + 2 * j + 1 : routes_total + 2 * j + 2]
        peak = jnp.maximum(c0, c1)
        e0 = jnp.exp(c0 - peak)
        e1 = jnp.exp(c1 - peak)
        mix.append((e0 / (e0 + e1), e1 / (e0 + e1)))
    rows_ref[...] = jnp.zeros_like(rows_ref)

    def put(i, value):
        rows_ref[i : i + 1, :] = value

    for k in range(2):
        put(k, gate[k])
        put(2 + k, column[k].astype(F32))
        copy = (route[k] == experts + 1).astype(F32)
        con = [(route[k] == experts + 2 + j).astype(F32) for j in range(2)]
        put(4 + k, copy + con[0] * mix[0][0] + con[1] * mix[1][0])
        put(6 + 2 * k, con[0] * mix[0][1])
        put(7 + 2 * k, con[1] * mix[1][1])
        put(10 + 2 * k, mix[k][0])
        put(11 + 2 * k, mix[k][1])
        put(14 + k, route[k].astype(F32))
    col_ref[...] = jnp.zeros_like(col_ref)
    col_ref[0:16, :] = rows_ref[...]

    def turn(c, carry):
        at = pl.multiple_of(c * chunk, chunk)
        cols_ref[pl.ds(at, chunk), :] = col_ref[:, pl.ds(at, chunk)].T
        return carry

    lax.fori_loop(0, length // chunk, turn, 0)

    piece = 176

    def dispatch(c, carry):
        at = pl.multiple_of(c * piece, 16)
        slot = at + iota((piece, 1), 0)
        col0 = rows_ref[2:3, :].astype(jnp.int32)
        col1 = rows_ref[3:4, :].astype(jnp.int32)
        m0 = slot == col0
        m1 = slot == col1
        pick = jnp.where(m0 | m1, 1.0, 0.0).astype(BF)
        weight = jnp.sum(
            jnp.where(m0, rows_ref[0:1, :], 0.0) + jnp.where(m1, rows_ref[1:2, :], 0.0),
            axis=1,
            keepdims=True,
        )
        send_ref[pl.ds(at, piece), :width] = nn(pick, n_ref[...]).astype(BF)
        send_ref[pl.ds(at, piece), width:] = (nn(pick, og_ref[...]) * weight).astype(BF)
        return carry

    lax.fori_loop(0, slots // piece, dispatch, 0)


def mid(tid, hidden, mine, other, gain, joint, prev, routes, og):
    length, width = hidden.shape
    experts = prev.shape[0] - 4
    slots = experts * (CAP // 2)
    return pl.pallas_call(
        mid_body,
        in_specs=[SMEM] + [pl.BlockSpec(memory_space=pltpu.VMEM)] * 8,
        out_specs=[pl.BlockSpec(memory_space=pltpu.VMEM)] * 5,
        out_shape=[
            jax.ShapeDtypeStruct((length, width), F32),
            jax.ShapeDtypeStruct((length, width), BF),
            jax.ShapeDtypeStruct((slots, 2 * width), BF),
            jax.ShapeDtypeStruct((16, length), F32),
            jax.ShapeDtypeStruct((length, 128), F32),
        ],
        scratch_shapes=[pltpu.VMEM((16, length), F32), pltpu.VMEM((128, length), F32)],
        compiler_params=params(),
        cost_estimate=cost(4 * slots * length * width, 16 << 20),
        name="mid",
    )(tid, hidden, mine, other, gain, joint, prev, routes, og)


def expert_body(
    own_ref, oth_ref, wg_ref, wu_ref, wd_ref, yown_ref, yoth_ref, grad_ref,
    x_ref, hid_ref, gp_ref, up_ref, xt_ref, dt_ref, y_ref,
):
    half = own_ref.shape[0]
    width = own_ref.shape[1] // 2
    units = hid_ref.shape[1]
    slots = 2 * half
    x_ref[:half, :] = own_ref[...]
    x_ref[half:, :] = oth_ref[...]
    w_gate = wg_ref[...].reshape(width, units)
    w_up = wu_ref[...].reshape(width, units)
    w_down = wd_ref[...].reshape(width, units)
    piece = 352

    def forward(c, carry):
        at = pl.multiple_of(c * piece, 16)
        x = x_ref[pl.ds(at, piece), :width]
        dy = x_ref[pl.ds(at, piece), width:]
        gate = nn(x, w_gate)
        up = nn(x, w_up)
        hg = nn(dy, w_down)
        sig = jax.nn.sigmoid(gate)
        act = gate * sig
        hid = (act * up).astype(BF)
        gp = (hg * up * sig * (1.0 + gate * (1.0 - sig))).astype(BF)
        upg = (hg * act).astype(BF)
        hid_ref[pl.ds(at, piece), :] = hid
        gp_ref[pl.ds(at, piece), :] = gp
        up_ref[pl.ds(at, piece), :] = upg
        y_ref[pl.ds(at, piece), :width] = nt(hid, w_down).astype(BF)
        y_ref[pl.ds(at, piece), width:] = (nt(gp, w_gate) + nt(upg, w_up)).astype(BF)
        return carry

    lax.fori_loop(0, slots // piece, forward, 0)
    yown_ref[...] = y_ref[:half, :]
    yoth_ref[...] = y_ref[half:, :]

    def turn(c, carry):
        at = pl.multiple_of(c * 128, 128)
        xt_ref[:, pl.ds(at, 128)] = x_ref[pl.ds(at, 128), :width].T
        dt_ref[:, pl.ds(at, 128)] = x_ref[pl.ds(at, 128), width:].T
        return carry

    lax.fori_loop(0, slots // 128, turn, 0)
    tile = 256
    peers, three, share, _ = grad_ref.shape
    for m, (left, right) in enumerate(((xt_ref, gp_ref), (xt_ref, up_ref), (dt_ref, hid_ref))):

        def weight(c, carry, m=m, left=left, right=right):
            at = pl.multiple_of(c * tile, tile)
            value = nn(left[...], right[:, pl.ds(at, tile)]).astype(BF)
            grad_ref[:, m, :, pl.ds(at, tile)] = value.reshape(peers, share, tile)
            return carry

        lax.fori_loop(0, units // tile, weight, 0)


def experts_call(own, oth, weights):
    half, twice = own.shape
    peers, three, share, units = weights.shape
    width = twice // 2
    slots = 2 * half
    third = lambda m: pl.BlockSpec((peers, None, share, units), lambda i, m=m: (0, m, 0, 0))
    return pl.pallas_call(
        expert_body,
        grid=(1,),
        in_specs=[whole(own.shape), whole(oth.shape), third(0), third(1), third(2)],
        out_specs=[whole(own.shape), whole(own.shape), whole(weights.shape)],
        out_shape=[
            jax.ShapeDtypeStruct(own.shape, BF),
            jax.ShapeDtypeStruct(own.shape, BF),
            jax.ShapeDtypeStruct(weights.shape, BF),
        ],
        scratch_shapes=[
            pltpu.VMEM((slots, twice), BF),
            pltpu.VMEM((slots, units), BF),
            pltpu.VMEM((slots, units), BF),
            pltpu.VMEM((slots, units), BF),
            pltpu.VMEM((width, slots), BF),
            pltpu.VMEM((width, slots), BF),
            pltpu.VMEM((slots, twice), BF),
        ],
        compiler_params=params(),
        cost_estimate=cost(18 * slots * width * units, 22 << 20),
        name="experts",
    )(own, oth, weights, weights, weights)


def combine_body(
    own_ref, oth_ref, r_ref, n_ref, rows_ref, cols_ref, gain_ref, cvec_ref, joint_ref, og_ref,
    out_ref, prev_ref, rg_ref, ag_ref, small_ref,
    y_ref, fs_ref, red_ref, jg_ref, jf_ref,
):
    length, width = r_ref.shape
    half = own_ref.shape[0]
    routes_total = prev_ref.shape[0]
    experts = routes_total - 4
    chunk = 256
    y_ref[:half, :] = own_ref[...]
    y_ref[half:, :] = oth_ref[...]
    gain = gain_ref[...]
    cvec = [cvec_ref[j : j + 1, :] for j in range(2)]
    red_ref[...] = jnp.zeros_like(red_ref)

    def first(c, carry):
        at = pl.multiple_of(c * chunk, chunk)
        cols = cols_ref[pl.ds(at, chunk), :]
        col = lambda i: cols[:, i : i + 1]
        slot = iota((1, 2 * half), 1)
        p0 = jnp.where(slot == col(2).astype(jnp.int32), 1.0, 0.0)
        p1 = jnp.where(slot == col(3).astype(jnp.int32), 1.0, 0.0)
        fs_ref[pl.ds(at, chunk), :] = nn((p0 + p1).astype(BF), y_ref[:, width:])
        got = [nn(p.astype(BF), y_ref[:, :width]) for p in (p0, p1)]
        r = r_ref[pl.ds(at, chunk), :]
        inv = lax.rsqrt(jnp.mean(r * r, axis=-1, keepdims=True) + EPSILON)
        nf = r * inv * gain
        og = og_ref[pl.ds(at, chunk), :].astype(F32)
        out = r
        sums = []
        for k in range(2):
            pair = got[k] + col(4 + k) * nf
            pair = pair + col(6 + 2 * k) * cvec[0] + col(7 + 2 * k) * cvec[1]
            out = out + col(k) * pair
            sums.append(jnp.sum(og * pair, axis=-1, keepdims=True))
        out_ref[pl.ds(at, chunk), :] = out.astype(BF)
        sums.append(jnp.sum(og * nf, axis=-1, keepdims=True))
        for j in range(2):
            sums.append(jnp.sum(og * cvec[j], axis=-1, keepdims=True))
        lane = iota((1, 128), 1)
        packed = jnp.zeros((chunk, 128), F32)
        for i, value in enumerate(sums):
            packed = jnp.where(lane == i, value, packed)
        red_ref[0:8, pl.ds(at, chunk)] = packed.T[0:8]
        return carry

    lax.fori_loop(0, length // chunk, first, 0)

    row = lambda i: rows_ref[i : i + 1, :]
    gate = [row(0), row(1)]
    route = [row(14).astype(jnp.int32), row(15).astype(jnp.int32)]
    sums = [red_ref[i : i + 1, :] for i in range(5)]
    both = gate[0] * sums[0] + gate[1] * sums[1]
    chosen = [gate[k] * (sums[k] - both) for k in range(2)]
    rid = iota((routes_total, length), 0)
    prev = jnp.where(rid == route[0], chosen[0], 0.0) + jnp.where(rid == route[1], chosen[1], 0.0)
    prev_ref[...] = prev
    jf_ref[0:routes_total, :] = prev
    weight_at = lambda r: (
        jnp.where(route[0] == r, gate[0], 0.0) + jnp.where(route[1] == r, gate[1], 0.0)
    )
    direct = weight_at(experts + 1)
    vec_rows = []
    for j in range(2):
        m0, m1 = row(10 + 2 * j), row(11 + 2 * j)
        weight = weight_at(experts + 2 + j)
        g0 = weight * sums[2]
        g1 = weight * sums[3 + j]
        mean = m0 * g0 + m1 * g1
        jf_ref[routes_total + 2 * j : routes_total + 2 * j + 1, :] = m0 * (g0 - mean)
        jf_ref[routes_total + 2 * j + 1 : routes_total + 2 * j + 2, :] = m1 * (g1 - mean)
        direct = direct + m0 * weight
        vec_rows.append(m1 * weight)
    jg_ref[...] = jf_ref[...].astype(BF)
    red_ref[8:9, :] = direct
    small_ref[...] = jnp.zeros_like(small_ref)
    small_ref[0:16, :] = nn(jg_ref[...], n_ref[...])
    vec = jnp.concatenate(vec_rows, axis=0)
    high = vec.astype(BF).astype(F32)
    lhs = jnp.concatenate([high, vec - high, jnp.zeros((12, length), F32)], axis=0).astype(BF)
    parts = nn(lhs, og_ref[...])
    small_ref[16:18, :] = parts[0:2] + parts[2:4]

    def second(c, carry):
        at = pl.multiple_of(c * chunk, chunk)
        direct = red_ref[:, pl.ds(at, chunk)].T[:, 8:9]
        og = og_ref[pl.ds(at, chunk), :].astype(F32)
        r = r_ref[pl.ds(at, chunk), :]
        inv = lax.rsqrt(jnp.mean(r * r, axis=-1, keepdims=True) + EPSILON)
        mg = fs_ref[pl.ds(at, chunk), :] + tn(jg_ref[:, pl.ds(at, chunk)], joint_ref[...])
        mg = mg + direct * og
        small_ref[18:19, :] += jnp.sum(mg * r * inv, axis=0, keepdims=True)
        scaled = mg * gain
        rg = og + inv * scaled - r * (inv * inv * inv) * jnp.mean(
            scaled * r, axis=-1, keepdims=True
        )
        rg_ref[pl.ds(at, chunk), :] = rg
        ag_ref[pl.ds(at, chunk), :] = rg.astype(BF)
        return carry

    lax.fori_loop(0, length // chunk, second, 0)


def combine(own, oth, r, n, rows, cols, gain, cvec, joint, og):
    length, width = r.shape
    routes_total = joint.shape[0] - 4
    slots = 2 * own.shape[0]
    vmem = pl.BlockSpec(memory_space=pltpu.VMEM)
    return pl.pallas_call(
        combine_body,
        in_specs=[vmem] * 10,
        out_specs=[vmem] * 5,
        out_shape=[
            jax.ShapeDtypeStruct((length, width), BF),
            jax.ShapeDtypeStruct((routes_total, length), F32),
            jax.ShapeDtypeStruct((length, width), F32),
            jax.ShapeDtypeStruct((length, width), BF),
            jax.ShapeDtypeStruct((24, width), F32),
        ],
        scratch_shapes=[
            pltpu.VMEM((slots, 2 * width), BF),
            pltpu.VMEM((length, width), F32),
            pltpu.VMEM((128, length), F32),
            pltpu.VMEM((16, length), BF),
            pltpu.VMEM((16, length), F32),
        ],
        compiler_params=params(),
        cost_estimate=cost(6 * slots * length * width, 22 << 20),
        name="combine",
    )(own, oth, r, n, rows, cols, gain, cvec, joint, og)


def final_body(h_ref, gain_ref, rg_ref, a_ref, b_ref, out_ref, grad_ref):
    @pl.when(pl.program_id(0) == 0)
    def _():
        grad_ref[...] = jnp.zeros_like(grad_ref)

    h = h_ref[...].astype(F32)
    inv = lax.rsqrt(jnp.mean(h * h, axis=-1, keepdims=True) + EPSILON)
    up = a_ref[...].astype(F32) + b_ref[...].astype(F32)
    grad_ref[0:1, :] += jnp.sum(up * h * inv, axis=0, keepdims=True)
    scaled = up * gain_ref[...]
    grad = inv * scaled - h * (inv * inv * inv) * jnp.mean(scaled * h, axis=-1, keepdims=True)
    out_ref[...] = (rg_ref[...] + grad).astype(BF)


def final(hidden, gain, rg, mine, other):
    length, width = hidden.shape
    blk = 256
    row = pl.BlockSpec((blk, width), lambda i: (i, 0))
    return pl.pallas_call(
        final_body,
        grid=(length // blk,),
        in_specs=[row, whole((1, width)), row, row, row],
        out_specs=[row, whole((8, width))],
        out_shape=[
            jax.ShapeDtypeStruct((length, width), BF),
            jax.ShapeDtypeStruct((8, width), F32),
        ],
        compiler_params=params(),
        cost_estimate=cost(20 * length * width, 9 << 20),
        name="final",
    )(hidden, gain, rg, mine, other)


def exchange(values, groups=None):
    return lax.all_to_all(
        values, "expert", split_axis=0, concat_axis=0, tiled=True, axis_index_groups=groups
    )


def swap(values):
    return lax.ppermute(values, "tensor", [(0, 1), (1, 0)])


def local(
    hidden_in, w_qkv, w_out, gain_in, gain_mid, w_router, w_const, const_vec,
    w_gate, w_up, w_down, prev_logits, routes, doc_ids, span_start, span_len, d_output,
):
    length, width = hidden_in.shape
    experts, share, units = w_gate.shape
    inner = w_qkv.shape[2]
    peers = lax.axis_size("expert")
    copies = peers // experts
    groups = [[g * experts + e for e in range(experts)] for g in range(copies)]
    routes_total = w_router.shape[1]

    stacked = jnp.stack([w_gate, w_up, w_down], axis=1).reshape(1, experts, 3 * share, units)
    sent = jnp.broadcast_to(stacked, (copies,) + stacked.shape[1:])
    weights = exchange(sent.reshape(peers, 3 * share, units)).reshape(peers, 3, share, units)
    fast = share % 16 == 0
    if not fast:
        weights = weights.transpose(1, 0, 2, 3).reshape(1, 3, width, units)

    lane = np.arange(128)
    frequency = 10000.0 ** (-jnp.asarray(lane % (HD // 2)).astype(F32) / (HD // 2))
    phase = jnp.arange(length).astype(F32)[:, None] * frequency[None, :]
    cos = jnp.cos(phase)
    sin = jnp.where((lane % HD < HD // 2)[None, :], -jnp.sin(phase), jnp.sin(phase))
    cuts = jnp.sum(doc_ids[None, :] < jnp.arange(1, 4)[:, None], axis=1, dtype=jnp.int32)
    meta = jnp.concatenate(
        [span_start[0], span_start[0] + span_len[0], cuts, jnp.zeros((1,), jnp.int32)]
    )

    w3 = w_qkv.transpose(1, 0, 2)
    normed_in, q, k, v = qkv(hidden_in, gain_in.reshape(1, width), w3, cos, sin)
    context, lse = attend(meta, q, k, v)
    attended = jnp.dot(context, w_out, preferred_element_type=F32)
    joint = jnp.concatenate([w_router.T, w_const.T], axis=0)
    tid = lax.axis_index("tensor").astype(jnp.int32).reshape(1)
    r, n, send, rows, cols = mid(
        tid, hidden_in, attended, swap(attended), gain_mid.reshape(1, width), joint,
        prev_logits.T, routes.T, d_output,
    )

    half = CAP // 2
    got = exchange(send.reshape(experts, half, 2 * width), groups).reshape(send.shape)
    y_own, y_oth, grads = experts_call(got, swap(got), weights)
    summed = y_own + swap(y_oth)
    back = exchange(summed.reshape(experts, half, 2 * width), groups).reshape(send.shape)
    if not fast:
        grads = grads.reshape(3, peers, share, units).transpose(1, 0, 2, 3)
    parted = exchange(grads.reshape(peers, 3 * share, units))

    output, prev_grad, rg, ag, small = combine(
        back, swap(back), r, n, rows, cols, gain_mid.reshape(1, width), const_vec, joint, d_output
    )
    pq, pk, pv = attend_back(meta, q, k, v, context, lse, ag, w_out, cos, sin)
    normed_grad = nt(pq, w3[0]) + nt(pk, w3[1]) + nt(pv, w3[2])
    normed_grad = normed_grad.astype(BF)
    grad_input, gain_grad = final(
        hidden_in, gain_in.reshape(1, width), rg, normed_grad, swap(normed_grad)
    )

    shared = [tn(normed_in, g).astype(BF).reshape(peers, share, inner) for g in (pq, pk, pv)]
    shared.append(tn(ag, context).astype(BF).reshape(peers, share, inner))
    shared = exchange(jnp.concatenate(shared, axis=1)).reshape(peers, 4, share, inner)
    shared = jnp.sum(shared.astype(F32), axis=0)
    small = jnp.concatenate([small[:19], gain_grad[0:1], small[20:]], axis=0)
    small = small.reshape(24, peers, share).transpose(1, 0, 2)
    small = jnp.sum(exchange(small), axis=0)

    parted = jnp.sum(
        parted.reshape(copies, experts, 3, share, units).astype(F32), axis=0
    )
    return (
        output,
        grad_input,
        prev_grad.T,
        shared[0:3].transpose(1, 0, 2),
        shared[3].T,
        small[19],
        small[18],
        small[0:routes_total].T,
        small[routes_total : routes_total + 4].T,
        small[16:18],
        parted[:, 0],
        parted[:, 1],
        parted[:, 2],
    )


def solution(mesh):
    rows = P("expert", None)
    expert_spec = P(None, "expert", "tensor")
    return jax.shard_map(
        local,
        mesh=mesh,
        in_specs=(
            rows, P(None, None, "tensor"), P("tensor", None), P(), P(), P(), P(), P(),
            expert_spec, expert_spec, expert_spec, rows, rows, P("expert"), rows, rows, rows,
        ),
        out_specs=(
            rows, rows, rows, P("expert", None, "tensor"), P("tensor", "expert"),
            P("expert"), P("expert"), rows, rows, P(None, "expert"),
            expert_spec, expert_spec, expert_spec,
        ),
        check_vma=False,
    )
```

```python
import functools

import jax
import jax.numpy as jnp
import numpy as np
from jax import lax
from jax.experimental import pallas as pl
from jax.experimental.pallas import tpu as pltpu
from jax.sharding import PartitionSpec as P

HD = 64
CAP = 176
PARTS = 2
EPSILON = 1e-06
BF = jnp.bfloat16
F32 = jnp.float32
NEG = -1e30
VMEM_LIMIT = 56 * 1024 * 1024


def nn(a, b):
    return lax.dot_general(a, b, (((1,), (0,)), ((), ())), preferred_element_type=F32)


def nt(a, b):
    return lax.dot_general(a, b, (((1,), (1,)), ((), ())), preferred_element_type=F32)


def tn(a, b):
    return lax.dot_general(a, b, (((0,), (0,)), ((), ())), preferred_element_type=F32)


def iota(shape, dim):
    return lax.broadcasted_iota(jnp.int32, shape, dim)


def params(**kw):
    return pltpu.CompilerParams(vmem_limit_bytes=VMEM_LIMIT, **kw)


def cost(flops, nbytes, trans=0):
    return pl.CostEstimate(flops=int(flops) // 1000, bytes_accessed=int(nbytes) // 1000, transcendentals=0)


def whole(shape):
    return pl.BlockSpec(shape, lambda *_: (0,) * len(shape))


SMEM = pl.BlockSpec(memory_space=pltpu.SMEM)


def swap_halves(values):
    width = values.shape[1]
    half = HD // 2
    lane = iota(values.shape, 1)
    ahead = pltpu.roll(values, width - half, 1)
    behind = pltpu.roll(values, half, 1)
    return jnp.where(lax.rem(lane, HD) < half, ahead, behind)


def qkv_body(h_ref, gain_ref, w_ref, cos_ref, sin_ref, n_ref, q_ref, k_ref, v_ref):
    h = h_ref[...].astype(F32)
    inv = lax.rsqrt(jnp.mean(h * h, axis=-1, keepdims=True) + EPSILON)
    normed = (h * inv * gain_ref[...]).astype(BF)
    n_ref[...] = normed
    copies = q_ref.shape[1] // 128
    cos = jnp.concatenate([cos_ref[...]] * copies, axis=1)
    sin = jnp.concatenate([sin_ref[...]] * copies, axis=1)
    q = nn(normed, w_ref[0])
    q_ref[...] = ((q * cos + swap_halves(q) * sin) * (HD**-0.5)).astype(BF)
    k = nn(normed, w_ref[1])
    k_ref[...] = (k * cos + swap_halves(k) * sin).astype(BF)
    v_ref[...] = nn(normed, w_ref[2]).astype(BF)


def qkv(hidden, gain, w3, cos, sin):
    length, width = hidden.shape
    inner = w3.shape[2]
    blk = 256
    row = lambda n: pl.BlockSpec((blk, n), lambda i: (i, 0))
    return pl.pallas_call(
        qkv_body,
        grid=(length // blk,),
        in_specs=[row(width), whole((1, width)), whole(w3.shape), row(128), row(128)],
        out_specs=[row(width), row(inner), row(inner), row(inner)],
        out_shape=[jax.ShapeDtypeStruct((length, width), BF)]
        + [jax.ShapeDtypeStruct((length, inner), BF)] * 3,
        compiler_params=params(),
        cost_estimate=cost(2 * length * width * inner * 3, 10 << 20),
        name="qkv",
    )(hidden, gain, w3, cos, sin)


def document_of(position, meta_ref):
    doc = jnp.zeros(position.shape, jnp.int32)
    for j in range(3):
        doc = doc + (position >= meta_ref[4 + j]).astype(jnp.int32)
    return doc


def span_of(position, meta_ref):
    span = jnp.zeros(position.shape, jnp.int32)
    for j in range(PARTS):
        inside = (position >= meta_ref[j]) & (position < meta_ref[2 + j])
        span = jnp.where(inside, span + (j + 1), span)
    return span


def mask_bias(query_pos, key_pos, meta_ref):
    query_span = span_of(query_pos, meta_ref)
    query_span = jnp.where(query_span == 0, -1, query_span)
    key_span = span_of(key_pos, meta_ref)
    same_doc = document_of(query_pos, meta_ref) == document_of(key_pos, meta_ref)
    seen = same_doc & ((key_pos <= query_pos) | (query_span == key_span))
    return jnp.where(seen, 0.0, NEG)


def attend_body(meta_ref, q_ref, k_ref, v_ref, ctx_ref, lse_ref, bias_ref):
    block = pl.program_id(0)
    pair = pl.program_id(1)
    rows, total = bias_ref.shape
    chunk = 256

    def run(keys):
        @pl.when(pair == 0)
        def _():
            for c in range(rows // chunk):
                qpos = block * rows + c * chunk + iota((chunk, 1), 0)
                kpos = iota((1, keys), 1)
                bias_ref[c * chunk : (c + 1) * chunk, :keys] = mask_bias(qpos, kpos, meta_ref)

        lane = iota((1, 128), 1)

        def step(c, carry):
            at = pl.multiple_of(c * chunk, chunk)
            q = q_ref[pl.ds(at, chunk), :]
            bias = bias_ref[pl.ds(at, chunk), :keys]
            k = k_ref[:keys, :]
            v = v_ref[:keys, :]
            outs = []
            for head in range(2):
                own = (lane // HD) == head
                qh = jnp.where(own, q, jnp.zeros_like(q))
                s = nt(qh, k) + bias
                top = jnp.max(s, axis=-1, keepdims=True)
                p = jnp.exp(s - top).astype(BF)
                mixed = nn(p, jnp.where(own, v, jnp.ones_like(v)))
                norm = pltpu.roll(mixed, HD, 1)
                outs.append((mixed / norm, top + jnp.log(norm)))
            first = lane < HD
            ctx_ref[pl.ds(at, chunk), :] = jnp.where(first, outs[0][0], outs[1][0]).astype(BF)
            lse = jnp.where(first, outs[0][1], outs[1][1]).T
            at2 = pl.multiple_of(block * rows + c * chunk, chunk)
            lse_ref[pl.ds(2 * pair, 1), pl.ds(at2, chunk)] = lse[0:1]
            lse_ref[pl.ds(2 * pair + 1, 1), pl.ds(at2, chunk)] = lse[HD : HD + 1]
            return carry

        lax.fori_loop(0, rows // chunk, step, 0)

    for b in range(PARTS):

        @pl.when(block == b)
        def _(b=b):
            run((b + 1) * rows)


def attend(meta, q, k, v):
    length, inner = q.shape
    pairs = inner // 128
    rows = length // PARTS
    heads8 = 8 * ((2 * pairs + 7) // 8)
    return pl.pallas_call(
        attend_body,
        grid=(PARTS, pairs),
        in_specs=[
            SMEM,
            pl.BlockSpec((rows, 128), lambda b, p: (b, p)),
            pl.BlockSpec((length, 128), lambda b, p: (0, p)),
            pl.BlockSpec((length, 128), lambda b, p: (0, p)),
        ],
        out_specs=[
            pl.BlockSpec((rows, 128), lambda b, p: (b, p)),
            whole((heads8, length)),
        ],
        out_shape=[
            jax.ShapeDtypeStruct((length, inner), BF),
            jax.ShapeDtypeStruct((heads8, length), F32),
        ],
        scratch_shapes=[pltpu.VMEM((rows, length), F32)],
        compiler_params=params(),
        cost_estimate=cost(4 * length * length * inner, 8 << 20, length * length * 6),
        name="attend",
    )(meta, q, k, v)


def attend_back_body(
    meta_ref, q_ref, k_ref, v_ref, ctx_ref, lse_ref, ag_ref, wo_ref, cos_ref, sin_ref,
    pq_ref, pk_ref, pv_ref, bias_ref, do_ref, delta_ref, dq0_ref, dq1_ref, *, first_pair
):
    pair = first_pair + pl.program_id(0)
    length = q_ref.shape[0]
    rows = length // PARTS
    chunk = 256
    lane = iota((1, 128), 1)
    first = lane < HD

    @pl.when(pair == first_pair)
    def _():
        def fill(c, carry):
            at = pl.multiple_of(c * chunk, chunk)
            kpos = at + iota((chunk, 1), 0)
            qpos = iota((1, length), 1)
            bias_ref[pl.ds(at, chunk), :] = mask_bias(qpos, kpos, meta_ref)
            return carry

        lax.fori_loop(0, length // chunk, fill, 0)

    def prepare(c, carry):
        at = pl.multiple_of(c * chunk, chunk)
        grad = nt(ag_ref[pl.ds(at, chunk), :], wo_ref[...]).astype(BF)
        do_ref[pl.ds(at, chunk), :] = grad
        prod = (grad.astype(F32) * ctx_ref[pl.ds(at, chunk), :].astype(F32)).T
        delta_ref[0:1, pl.ds(at, chunk)] = jnp.sum(prod[:HD], axis=0, keepdims=True)
        delta_ref[1:2, pl.ds(at, chunk)] = jnp.sum(prod[HD:], axis=0, keepdims=True)
        return carry

    lax.fori_loop(0, length // chunk, prepare, 0)
    dq0_ref[...] = jnp.zeros_like(dq0_ref)
    dq1_ref[...] = jnp.zeros_like(dq1_ref)

    def step(c, carry, start):
        count = length - start
        at = pl.multiple_of(c * chunk, chunk)
        k = k_ref[pl.ds(at, chunk), :]
        v = v_ref[pl.ds(at, chunk), :]
        bias = bias_ref[pl.ds(at, chunk), start:]
        q = q_ref[start:, :]
        grad = do_ref[start:, :]
        dks = []
        dvs = []
        for head in range(2):
            own = (lane // HD) == head
            kh = jnp.where(own, k, jnp.zeros_like(k))
            vh = jnp.where(own, v, jnp.zeros_like(v))
            lse = lse_ref[pl.ds(2 * pair + head, 1), start:]
            p = jnp.exp(nt(kh, q) + bias - lse)
            dvs.append(nn(p.astype(BF), grad))
            dp = nt(vh, grad)
            ds = (p * (dp - delta_ref[head : head + 1, start:])).astype(BF)
            dks.append(nn(ds, q))
            dq_ref = dq0_ref if head == 0 else dq1_ref
            dq_ref[start:, :] += tn(ds, k)
        dk = jnp.where(first, dks[0], dks[1])
        cos = cos_ref[pl.ds(at, chunk), :]
        sin = sin_ref[pl.ds(at, chunk), :]
        pk_ref[pl.ds(at, chunk), :] = (dk * cos - swap_halves(dk) * sin).astype(BF)
        pv_ref[pl.ds(at, chunk), :] = jnp.where(first, dvs[0], dvs[1]).astype(BF)
        return carry

    for b in range(PARTS):
        per = rows // chunk
        lax.fori_loop(b * per, (b + 1) * per, functools.partial(step, start=b * rows), 0)

    def finish(c, carry):
        at = pl.multiple_of(c * chunk, chunk)
        dq = jnp.where(first, dq0_ref[pl.ds(at, chunk), :], dq1_ref[pl.ds(at, chunk), :])
        dq = dq * (HD**-0.5)
        cos = cos_ref[pl.ds(at, chunk), :]
        sin = sin_ref[pl.ds(at, chunk), :]
        pq_ref[pl.ds(at, chunk), :] = (dq * cos - swap_halves(dq) * sin).astype(BF)
        return carry

    lax.fori_loop(0, length // chunk, finish, 0)


def attend_back(meta, q, k, v, ctx, lse, agrad, w_out, cos, sin, first_pair, pairs, weight=1):
    length = q.shape[0]
    inner = 128 * pairs
    width = agrad.shape[1]
    col = pl.BlockSpec((length, 128), lambda p: (0, first_pair + p))
    out = pl.BlockSpec((length, 128), lambda p: (0, p))
    return pl.pallas_call(
        functools.partial(attend_back_body, first_pair=first_pair),
        grid=(pairs,),
        in_specs=[
            SMEM, col, col, col, col, whole(lse.shape), whole((length, width)),
            pl.BlockSpec((128, width), lambda p: (first_pair + p, 0)),
            whole((length, 128)), whole((length, 128)),
        ],
        out_specs=[out, out, out],
        out_shape=[jax.ShapeDtypeStruct((length, inner), BF)] * 3,
        scratch_shapes=[
            pltpu.VMEM((length, length), F32),
            pltpu.VMEM((length, 128), BF),
            pltpu.VMEM((8, length), F32),
            pltpu.VMEM((length, 128), F32),
            pltpu.VMEM((length, 128), F32),
        ],
        compiler_params=params(),
        cost_estimate=cost(10 * length * length * inner * weight, 12 << 20),
        name="attend_back",
    )(meta, q, k, v, ctx, lse, agrad, w_out, cos, sin)


def route_body(where_ref, routes_ref, col_ref, *, blocks):
    length = routes_ref.shape[1]
    half = CAP // 2
    slots = blocks * half
    tid = where_ref[0]
    me = where_ref[1]
    route = [routes_ref[k : k + 1, :] for k in range(2)]
    rid = iota((16, length), 0)
    hot = ((rid == route[0]) | (rid == route[1])).astype(F32)
    blk = 256
    upper = (iota((blk, blk), 0) < iota((blk, blk), 1)).astype(BF)
    before = jnp.zeros((16, 1), F32)
    parts = []
    for c in range(length // blk):
        part = hot[:, c * blk : (c + 1) * blk]
        parts.append(nn(part.astype(BF), upper) + before)
        before = before + jnp.sum(part, axis=1, keepdims=True)
    count = jnp.concatenate(parts, axis=1)
    column = []
    for k in range(2):
        pos = jnp.sum(jnp.where(rid == route[k], count, 0.0), axis=0, keepdims=True)
        pos = pos.astype(jnp.int32)
        kept = (route[k] < blocks) & (pos < CAP)
        side = (pos >= half).astype(jnp.int32)
        block = route[k] ^ lax.rem(me, blocks) ^ (blocks // 2)
        col = jnp.where(side == tid, 0, slots) + block * half + pos - side * half
        column.append(jnp.where(kept, col, -1))
    col_ref[...] = jnp.concatenate(
        [column[0], column[1], jnp.zeros((6, length), jnp.int32)], axis=0
    )


def route_call(where, routes, blocks):
    length = routes.shape[1]
    return pl.pallas_call(
        functools.partial(route_body, blocks=blocks),
        in_specs=[SMEM, pl.BlockSpec(memory_space=pltpu.VMEM)],
        out_specs=pl.BlockSpec(memory_space=pltpu.VMEM),
        out_shape=jax.ShapeDtypeStruct((8, length), jnp.int32),
        compiler_params=params(),
        cost_estimate=cost(0, 1 << 16),
        name="route",
    )(where, routes)


def mid_body(
    h_ref, a_ref, b_ref, gain_ref, joint_ref, prev_ref, routes_ref, place_ref, og_ref,
    r_ref, n_ref, rows_ref, cols_ref, *rest,
):
    send_refs, (lg_ref, col_ref) = rest[:-2], rest[-2:]
    length = h_ref.shape[0]
    routes_total = prev_ref.shape[0]
    experts = routes_total - 4
    half = CAP // 2
    chunk = 256

    def norm(c, carry):
        at = pl.multiple_of(c * chunk, chunk)
        r = h_ref[pl.ds(at, chunk), :].astype(F32) + (
            a_ref[pl.ds(at, chunk), :] + b_ref[pl.ds(at, chunk), :]
        )
        r_ref[pl.ds(at, chunk), :] = r
        inv = lax.rsqrt(jnp.mean(r * r, axis=-1, keepdims=True) + EPSILON)
        normed = (r * inv * gain_ref[...]).astype(BF)
        n_ref[pl.ds(at, chunk), :] = normed
        lg_ref[:, pl.ds(at, chunk)] = nt(joint_ref[...], normed)
        return carry

    lax.fori_loop(0, length // chunk, norm, 0)

    lg = lg_ref[...]
    logits = lg[:routes_total] + prev_ref[...]
    route = [routes_ref[k : k + 1, :] for k in range(2)]
    rid = iota((routes_total, length), 0)
    chosen = [jnp.sum(jnp.where(rid == r, logits, 0.0), axis=0, keepdims=True) for r in route]
    top = jnp.maximum(chosen[0], chosen[1])
    raised = [jnp.exp(c - top) for c in chosen]
    total = raised[0] + raised[1]
    gate = [e / total for e in raised]
    mix = []
    for j in range(2):
        c0 = lg[routes_total + 2 * j : routes_total + 2 * j + 1]
        c1 = lg[routes_total + 2 * j + 1 : routes_total + 2 * j + 2]
        peak = jnp.maximum(c0, c1)
        e0 = jnp.exp(c0 - peak)
        e1 = jnp.exp(c1 - peak)
        mix.append((e0 / (e0 + e1), e1 / (e0 + e1)))
    column = [place_ref[k : k + 1, :] for k in range(2)]

    def put(i, value):
        rows_ref[i : i + 1, :] = value

    for k in range(2):
        put(k, gate[k])
        put(2 + k, column[k].astype(F32))
        copy = (route[k] == experts + 1).astype(F32)
        con = [(route[k] == experts + 2 + j).astype(F32) for j in range(2)]
        put(4 + k, copy + con[0] * mix[0][0] + con[1] * mix[1][0])
        put(6 + 2 * k, con[0] * mix[0][1])
        put(7 + 2 * k, con[1] * mix[1][1])
        put(10 + 2 * k, mix[k][0])
        put(11 + 2 * k, mix[k][1])
        put(14 + k, route[k].astype(F32))
    col_ref[...] = jnp.zeros_like(col_ref)
    col_ref[0:16, :] = rows_ref[...]

    def turn(c, carry):
        at = pl.multiple_of(c * chunk, chunk)
        cols_ref[pl.ds(at, chunk), :] = col_ref[:, pl.ds(at, chunk)].T
        return carry

    lax.fori_loop(0, length // chunk, turn, 0)

    width = h_ref.shape[1]
    for b, ref in enumerate(send_refs):
        slot = b * half + iota((half, 1), 0)
        match = [slot == c for c in column]
        pick = jnp.where(match[0] | match[1], 1.0, 0.0).astype(BF)
        weight = jnp.sum(
            jnp.where(match[0], gate[0], 0.0) + jnp.where(match[1], gate[1], 0.0),
            axis=1,
            keepdims=True,
        )
        ref[:, :width] = nn(pick, n_ref[...]).astype(BF)
        ref[:, width:] = (nn(pick, og_ref[...]) * weight).astype(BF)


def mid(hidden, mine, other, gain, joint, prev, routes, place, og):
    length, width = hidden.shape
    blocks = prev.shape[0] - 4
    vmem = pl.BlockSpec(memory_space=pltpu.VMEM)
    return pl.pallas_call(
        mid_body,
        in_specs=[vmem] * 9,
        out_specs=[vmem] * (4 + blocks),
        out_shape=[
            jax.ShapeDtypeStruct((length, width), F32),
            jax.ShapeDtypeStruct((length, width), BF),
            jax.ShapeDtypeStruct((16, length), F32),
            jax.ShapeDtypeStruct((length, 128), F32),
        ]
        + [jax.ShapeDtypeStruct((CAP // 2, 2 * width), BF)] * blocks,
        scratch_shapes=[pltpu.VMEM((16, length), F32), pltpu.VMEM((128, length), F32)],
        compiler_params=params(),
        cost_estimate=cost(2 * blocks * (CAP // 2) * length * width, 14 << 20),
        name="mid",
    )(hidden, mine, other, gain, joint, prev, routes, place, og)


def third(weights, m):
    peers, _, share, units = weights.shape
    return pl.BlockSpec((peers, None, share, units), lambda *_: (0, m, 0, 0))


def units_of(x, dy, weight_refs, base=None):
    width = x.shape[1]
    w_gate, w_up, w_down = (ref[...].reshape(width, ref.shape[2]) for ref in weight_refs)
    gate = nn(x, w_gate)
    up = nn(x, w_up)
    hg = nn(dy, w_down)
    sig = jax.nn.sigmoid(gate)
    act = gate * sig
    hid = (act * up).astype(BF)
    gp = (hg * up * sig * (1.0 + gate * (1.0 - sig))).astype(BF)
    upg = (hg * act).astype(BF)
    return hid, gp, upg, nt(hid, w_down), nt(gp, w_gate) + nt(upg, w_up)


def ffn_first_body(*refs):
    count = len(refs) - 10
    block_refs, weight_refs = refs[:count], refs[count : count + 3]
    x_ref, dy_ref, hid_ref, gp_ref, up_ref, y_ref, xs_ref = refs[count + 3 :]
    step = pl.program_id(0)
    size = block_refs[0].shape[0]
    piece, width = x_ref.shape

    @pl.when(step == 0)
    def _():
        for b in range(count):
            xs_ref[b * size : (b + 1) * size, :] = block_refs[b][...]

    at = pl.multiple_of(step * piece, 16)
    x = xs_ref[pl.ds(at, piece), :width]
    dy = xs_ref[pl.ds(at, piece), width:]
    x_ref[...] = x
    dy_ref[...] = dy
    hid_ref[...], gp_ref[...], up_ref[...], out, back = units_of(x, dy, weight_refs)
    y_ref[:, :width] = out.astype(BF)
    y_ref[:, width:] = back.astype(BF)


def ffn_first(blocks, trio):
    peers, _, share, units = trio.shape
    size, twice = blocks[0].shape
    width = twice // 2
    slots = size * len(blocks)
    piece = slots // 4
    row = lambda n: pl.BlockSpec((piece, n), lambda i: (i, 0))
    widths = (width, width, units, units, units, twice)
    return pl.pallas_call(
        ffn_first_body,
        grid=(4,),
        in_specs=[whole(a.shape) for a in blocks] + [third(trio, m) for m in range(3)],
        out_specs=[row(n) for n in widths],
        out_shape=[jax.ShapeDtypeStruct((slots, n), BF) for n in widths],
        scratch_shapes=[pltpu.VMEM((slots, twice), BF)],
        compiler_params=params(),
        cost_estimate=pl.CostEstimate(flops=40_355_000_000, bytes_accessed=1000, transcendentals=0),
        name="ffn_first",
    )(*blocks, trio, trio, trio)


def ffn_second_body(x_ref, dy_ref, part_ref, *refs):
    weight_refs, (hid_ref, gp_ref, up_ref, y_ref) = refs[:3], refs[3:]
    width = x_ref.shape[1]
    hid_ref[...], gp_ref[...], up_ref[...], out, back = units_of(
        x_ref[...], dy_ref[...], weight_refs
    )
    y_ref[:, :width] = (out + part_ref[:, :width].astype(F32)).astype(BF)
    y_ref[:, width:] = (back + part_ref[:, width:].astype(F32)).astype(BF)


def ffn_second(side, x, dy, part, trio):
    peers, _, share, units = trio.shape
    slots, width = x.shape
    piece = slots // 4
    row = lambda n: pl.BlockSpec((piece, n), lambda i: (2 * side + i, 0))
    out = lambda n: pl.BlockSpec((piece, n), lambda i: (i, 0))
    widths = (units, units, units, 2 * width)
    return pl.pallas_call(
        ffn_second_body,
        grid=(2,),
        in_specs=[row(width), row(width), row(2 * width)] + [third(trio, m) for m in range(3)],
        out_specs=[out(n) for n in widths],
        out_shape=[jax.ShapeDtypeStruct((slots // 2, n), BF) for n in widths],
        compiler_params=params(),
        cost_estimate=cost(7 * slots * width * units, 12 << 20),
        name="ffn_second",
    )(x, dy, part, trio, trio, trio)


def learn_body(x_ref, dy_ref, *refs):
    saved, (out_ref, xt_ref, dt_ref, g_ref) = refs[:9], refs[9:]
    units = g_ref.shape[1]
    peers, _, share, _ = out_ref.shape
    tile = 256

    def turn(c, carry):
        at = pl.multiple_of(c * 128, 128)
        xt_ref[:, pl.ds(at, 128)] = x_ref[pl.ds(at, 128), :].T
        dt_ref[:, pl.ds(at, 128)] = dy_ref[pl.ds(at, 128), :].T
        return carry

    lax.fori_loop(0, x_ref.shape[0] // 128, turn, 0)
    for m, left in ((2, dt_ref), (0, xt_ref), (1, xt_ref)):
        kind = (m + 1) % 3
        for part in range(2):
            if part == 0:
                right = saved[kind]
            else:
                right = g_ref
                half = g_ref.shape[0] // 2
                g_ref[:half, :] = saved[3 + kind][...]
                g_ref[half:, :] = saved[6 + kind][...]

            def step(c, carry, m=m, left=left, right=right, part=part):
                at = pl.multiple_of(c * tile, tile)
                value = nn(left[...], right[:, pl.ds(at, tile)]).astype(BF)
                value = value.reshape(peers, share, tile)
                out_ref[:, m, :, pl.ds(pl.multiple_of(part * units + at, tile), tile)] = value
                return carry

            lax.fori_loop(0, units // tile, step, 0)


def learn(x, dy, saved, peers):
    slots, width = x.shape
    units = saved[0].shape[1]
    vmem = pl.BlockSpec(memory_space=pltpu.VMEM)
    return pl.pallas_call(
        learn_body,
        in_specs=[vmem] * (2 + len(saved)),
        out_specs=vmem,
        out_shape=jax.ShapeDtypeStruct((peers, 3, width // peers, 2 * units), BF),
        scratch_shapes=[
            pltpu.VMEM((width, slots), BF),
            pltpu.VMEM((width, slots), BF),
            pltpu.VMEM((slots, units), BF),
        ],
        compiler_params=params(),
        cost_estimate=cost(12 * slots * width * units, 18 << 20),
        name="learn",
    )(x, dy, *saved)


def total_body(*refs):
    part_refs, outs = refs[:-3], refs[-3:]
    for m, out_ref in enumerate(outs):
        at = 0
        for ref in part_refs:
            value = ref[0, 0, m].astype(F32)
            for g in range(1, ref.shape[0]):
                value = value + ref[g, 0, m].astype(F32)
            out_ref[0, :, at : at + value.shape[1]] = value
            at += value.shape[1]


def total_call(*parts):
    copies, experts, three, share, _ = parts[0].shape
    units = sum(p.shape[4] for p in parts)
    part = lambda p: pl.BlockSpec((copies, 1, three, share, p.shape[4]), lambda e: (0, e, 0, 0, 0))
    return pl.pallas_call(
        total_body,
        grid=(experts,),
        in_specs=[part(p) for p in parts],
        out_specs=[pl.BlockSpec((1, share, units), lambda e: (e, 0, 0))] * 3,
        out_shape=[jax.ShapeDtypeStruct((experts, share, units), F32)] * 3,
        compiler_params=params(),
        cost_estimate=cost(30_000_000_000_000, 0),
        name="total",
    )(*parts)


def join_body(a_ref, b_ref, *out_refs):
    half = out_refs[0].shape[0]
    for b, ref in enumerate(out_refs):
        at = b * half
        ref[...] = (
            a_ref[at : at + half, :].astype(F32) + b_ref[at : at + half, :].astype(F32)
        ).astype(BF)


def join(mine, other, blocks):
    half = mine.shape[0] // blocks
    vmem = pl.BlockSpec(memory_space=pltpu.VMEM)
    return pl.pallas_call(
        join_body,
        in_specs=[vmem] * 2,
        out_specs=[vmem] * blocks,
        out_shape=[jax.ShapeDtypeStruct((half, mine.shape[1]), BF)] * blocks,
        compiler_params=params(),
        cost_estimate=cost(mine.size, 6 * mine.size),
        name="join",
    )(mine, other)


def combine_body(*refs):
    count = len(refs) - 18
    block_refs = refs[:count]
    (r_ref, n_ref, rows_ref, cols_ref, gain_ref, cvec_ref, joint_ref, og_ref,
     out_ref, prev_ref, rg_ref, ag_ref, small_ref,
     y_ref, fs_ref, red_ref, jg_ref, jf_ref) = refs[count:]
    length, width = r_ref.shape
    half = y_ref.shape[0] // 2
    routes_total = prev_ref.shape[0]
    experts = routes_total - 4
    chunk = 256
    size = block_refs[0].shape[0]
    for b, ref in enumerate(block_refs):
        y_ref[b * size : (b + 1) * size, :] = ref[...]
    gain = gain_ref[...]
    cvec = [cvec_ref[j : j + 1, :] for j in range(2)]
    red_ref[...] = jnp.zeros_like(red_ref)

    def first(c, carry):
        at = pl.multiple_of(c * chunk, chunk)
        cols = cols_ref[pl.ds(at, chunk), :]
        col = lambda i: cols[:, i : i + 1]
        slot = iota((1, 2 * half), 1)
        p0 = jnp.where(slot == col(2).astype(jnp.int32), 1.0, 0.0)
        p1 = jnp.where(slot == col(3).astype(jnp.int32), 1.0, 0.0)
        fs_ref[pl.ds(at, chunk), :] = nn((p0 + p1).astype(BF), y_ref[:, width:])
        got = [nn(p.astype(BF), y_ref[:, :width]) for p in (p0, p1)]
        r = r_ref[pl.ds(at, chunk), :]
        inv = lax.rsqrt(jnp.mean(r * r, axis=-1, keepdims=True) + EPSILON)
        nf = r * inv * gain
        og = og_ref[pl.ds(at, chunk), :].astype(F32)
        out = r
        sums = []
        for k in range(2):
            pair = got[k] + col(4 + k) * nf
            pair = pair + col(6 + 2 * k) * cvec[0] + col(7 + 2 * k) * cvec[1]
            out = out + col(k) * pair
            sums.append(jnp.sum(og * pair, axis=-1, keepdims=True))
        out_ref[pl.ds(at, chunk), :] = out.astype(BF)
        sums.append(jnp.sum(og * nf, axis=-1, keepdims=True))
        for j in range(2):
            sums.append(jnp.sum(og * cvec[j], axis=-1, keepdims=True))
        lane = iota((1, 128), 1)
        packed = jnp.zeros((chunk, 128), F32)
        for i, value in enumerate(sums):
            packed = jnp.where(lane == i, value, packed)
        red_ref[0:8, pl.ds(at, chunk)] = packed.T[0:8]
        return carry

    lax.fori_loop(0, length // chunk, first, 0)

    row = lambda i: rows_ref[i : i + 1, :]
    gate = [row(0), row(1)]
    route = [row(14).astype(jnp.int32), row(15).astype(jnp.int32)]
    sums = [red_ref[i : i + 1, :] for i in range(5)]
    both = gate[0] * sums[0] + gate[1] * sums[1]
    chosen = [gate[k] * (sums[k] - both) for k in range(2)]
    rid = iota((routes_total, length), 0)
    prev = jnp.where(rid == route[0], chosen[0], 0.0) + jnp.where(rid == route[1], chosen[1], 0.0)
    prev_ref[...] = prev
    jf_ref[0:routes_total, :] = prev
    weight_at = lambda r: (
        jnp.where(route[0] == r, gate[0], 0.0) + jnp.where(route[1] == r, gate[1], 0.0)
    )
    direct = weight_at(experts + 1)
    vec_rows = []
    for j in range(2):
        m0, m1 = row(10 + 2 * j), row(11 + 2 * j)
        weight = weight_at(experts + 2 + j)
        g0 = weight * sums[2]
        g1 = weight * sums[3 + j]
        mean = m0 * g0 + m1 * g1
        jf_ref[routes_total + 2 * j : routes_total + 2 * j + 1, :] = m0 * (g0 - mean)
        jf_ref[routes_total + 2 * j + 1 : routes_total + 2 * j + 2, :] = m1 * (g1 - mean)
        direct = direct + m0 * weight
        vec_rows.append(m1 * weight)
    jg_ref[...] = jf_ref[...].astype(BF)
    red_ref[8:9, :] = direct
    small_ref[...] = jnp.zeros_like(small_ref)
    small_ref[0:16, :] = nn(jg_ref[...], n_ref[...])
    vec = jnp.concatenate(vec_rows, axis=0)
    high = vec.astype(BF).astype(F32)
    lhs = jnp.concatenate([high, vec - high, jnp.zeros((12, length), F32)], axis=0).astype(BF)
    parts = nn(lhs, og_ref[...])
    small_ref[16:18, :] = parts[0:2] + parts[2:4]

    def second(c, carry):
        at = pl.multiple_of(c * chunk, chunk)
        direct = red_ref[:, pl.ds(at, chunk)].T[:, 8:9]
        og = og_ref[pl.ds(at, chunk), :].astype(F32)
        r = r_ref[pl.ds(at, chunk), :]
        inv = lax.rsqrt(jnp.mean(r * r, axis=-1, keepdims=True) + EPSILON)
        mg = fs_ref[pl.ds(at, chunk), :] + tn(jg_ref[:, pl.ds(at, chunk)], joint_ref[...])
        mg = mg + direct * og
        small_ref[18:19, :] += jnp.sum(mg * r * inv, axis=0, keepdims=True)
        scaled = mg * gain
        rg = og + inv * scaled - r * (inv * inv * inv) * jnp.mean(
            scaled * r, axis=-1, keepdims=True
        )
        rg_ref[pl.ds(at, chunk), :] = rg
        ag_ref[pl.ds(at, chunk), :] = rg.astype(BF)
        return carry

    lax.fori_loop(0, length // chunk, second, 0)


def combine(blocks, r, n, rows, cols, gain, cvec, joint, og):
    length, width = r.shape
    routes_total = joint.shape[0] - 4
    slots = len(blocks) * blocks[0].shape[0]
    vmem = pl.BlockSpec(memory_space=pltpu.VMEM)
    return pl.pallas_call(
        combine_body,
        in_specs=[vmem] * (len(blocks) + 8),
        out_specs=[vmem] * 5,
        out_shape=[
            jax.ShapeDtypeStruct((length, width), BF),
            jax.ShapeDtypeStruct((routes_total, length), F32),
            jax.ShapeDtypeStruct((length, width), F32),
            jax.ShapeDtypeStruct((length, width), BF),
            jax.ShapeDtypeStruct((24, width), F32),
        ],
        scratch_shapes=[
            pltpu.VMEM((slots, 2 * width), BF),
            pltpu.VMEM((length, width), F32),
            pltpu.VMEM((128, length), F32),
            pltpu.VMEM((16, length), BF),
            pltpu.VMEM((16, length), F32),
        ],
        compiler_params=params(),
        cost_estimate=pl.CostEstimate(flops=92_240_000_000, bytes_accessed=1000, transcendentals=0),
        name="combine",
    )(*blocks, r, n, rows, cols, gain, cvec, joint, og)


def inward_body(*refs):
    grads, (w_ref, h_ref, ng_ref, gain_ref) = refs[:-4], refs[-4:]

    @pl.when(pl.program_id(0) == 0)
    def _():
        gain_ref[...] = jnp.zeros_like(gain_ref)

    up = 0.0
    at = 0
    for g in range(0, len(grads), 3):
        size = grads[g].shape[1]
        for c in range(3):
            up = up + nt(grads[g + c][...], w_ref[c, :, at : at + size])
        at += size
    up = up.astype(BF)
    ng_ref[...] = up
    h = h_ref[...].astype(F32)
    inv = lax.rsqrt(jnp.mean(h * h, axis=-1, keepdims=True) + EPSILON)
    gain_ref[0:1, :] += jnp.sum(up.astype(F32) * h * inv, axis=0, keepdims=True)


def inward(grads, w3, hidden):
    length, width = hidden.shape
    inner = w3.shape[2]
    blk = 256
    row = lambda n: pl.BlockSpec((blk, n), lambda i: (i, 0))
    return pl.pallas_call(
        inward_body,
        grid=(length // blk,),
        in_specs=[row(g.shape[1]) for g in grads] + [whole(w3.shape), row(width)],
        out_specs=[row(width), whole((8, width))],
        out_shape=[
            jax.ShapeDtypeStruct((length, width), BF),
            jax.ShapeDtypeStruct((8, width), F32),
        ],
        compiler_params=params(),
        cost_estimate=cost(6 * length * width * inner, 7 << 20),
        name="inward",
    )(*grads, w3, hidden)


def fold_place(j, peers):
    return (j & 1) * (peers // 2) + ((j >> 1) & 1) * (peers // 4) + (j >> 2)


def shared_body(where_ref, *refs, lefts, small):
    nleft = max(lefts) + 1
    left_refs = refs[:nleft]
    right_refs = refs[nleft : nleft + len(lefts)]
    keep_ref, send_ref, all_ref, t_ref = refs[-4:]
    half, rows, inner = keep_ref.shape
    peers = 2 * half
    length, width = left_refs[0].shape
    share = width // peers
    me = where_ref[1]
    places = [fold_place(p ^ me, peers) for p in range(peers)]
    done = -1
    group = 0
    for which, right in zip(lefts, right_refs):
        if which != done:

            def turn(c, carry, left=left_refs[which]):
                at = pl.multiple_of(c * 128, 128)
                t_ref[:, pl.ds(at, 128)] = left[pl.ds(at, 128), :].T
                return carry

            lax.fori_loop(0, length // 128, turn, 0)
            done = which
        value = nn(t_ref[...], right[...]).astype(BF)
        for at in range(0, right.shape[1], 128):
            row, lane = group * 128 // inner * share, group * 128 % inner
            for p in range(peers):
                all_ref[places[p], row : row + share, lane : lane + 128] = value[
                    p * share : (p + 1) * share, at : at + 128
                ]
            group += 1
    if small:
        small_ref, mine_ref, other_ref = refs[nleft + len(lefts) : -4]
        gain = mine_ref[0:1, :] + other_ref[0:1, :]
        table = small_ref[...]
        table = jnp.where(iota((table.shape[0], 1), 0) == 19, gain, table).astype(BF)
        for p in range(peers):
            all_ref[places[p], share:, :] = jnp.zeros((rows - share, inner), BF)
            all_ref[places[p], share : share + table.shape[0], 0:share] = table[
                :, p * share : (p + 1) * share
            ]
    keep_ref[...] = all_ref[:half]
    send_ref[...] = all_ref[half:]


def shared_call(where, lefts, which, rights, tail, inner, peers):
    length, width = lefts[0].shape
    share = width // peers
    total = sum(r.shape[1] for r in rights)
    rows = total // inner * share + (32 if tail else 0)
    vmem = pl.BlockSpec(memory_space=pltpu.VMEM)
    return pl.pallas_call(
        functools.partial(shared_body, lefts=which, small=bool(tail)),
        in_specs=[SMEM] + [vmem] * (len(lefts) + len(rights) + len(tail)),
        out_specs=[vmem] * 2,
        out_shape=[jax.ShapeDtypeStruct((peers // 2, rows, inner), BF)] * 2,
        scratch_shapes=[pltpu.VMEM((peers, rows, inner), BF), pltpu.VMEM((width, length), BF)],
        compiler_params=params(),
        cost_estimate=cost(2 * length * width * total, 4 << 20),
        name="shared",
    )(where, *lefts, *rights, *tail)


def gather_body(*refs):
    part_refs, outs = refs[:-7], refs[-7:]
    qkv_ref, wout_ref, router_ref, const_ref, cvec_ref, mid_ref, in_ref = outs
    total = part_refs[0][0].astype(F32)
    for ref in part_refs[1:]:
        total = total + ref[...].astype(F32)
    share, inner = wout_ref.shape
    pairs = inner // 128
    pick = lambda g: total[
        g * 128 // inner * share : g * 128 // inner * share + share,
        g * 128 % inner : g * 128 % inner + 128,
    ]
    for i in range(pairs):
        wout_ref[:, i * 128 : (i + 1) * 128] = pick(i)
    for c in range(3):
        for i in range(pairs):
            g = pairs + c * (pairs - 1) + i if i < pairs - 1 else pairs + 3 * (pairs - 1) + c
            qkv_ref[c, :, i * 128 : (i + 1) * 128] = pick(g)
    tail = total[4 * share :, 0:share]
    routes = router_ref.shape[0]
    router_ref[...] = tail[0:routes]
    const_ref[...] = tail[routes : routes + 4]
    cvec_ref[...] = tail[16:18]
    mid_ref[...] = tail[18:19]
    in_ref[...] = tail[19:20]


def gather(parts, routes, share, inner):
    vmem = pl.BlockSpec(memory_space=pltpu.VMEM)
    shapes = [(3, share, inner), (share, inner), (routes, share), (4, share), (2, share), (1, share), (1, share)]
    first = pl.BlockSpec((1,) + parts[0].shape[1:], lambda i: (0, 0, 0))
    return pl.pallas_call(
        gather_body,
        grid=(1,),
        in_specs=[first] + [whole(p.shape) for p in parts[1:]],
        out_specs=[whole(shape) for shape in shapes],
        out_shape=[jax.ShapeDtypeStruct(shape, F32) for shape in shapes],
        compiler_params=params(),
        cost_estimate=cost(4 * parts[1].size, 2 << 20),
        name="gather",
    )(*parts)


def final_body(h_ref, gain_ref, rg_ref, a_ref, b_ref, out_ref):
    h = h_ref[...].astype(F32)
    inv = lax.rsqrt(jnp.mean(h * h, axis=-1, keepdims=True) + EPSILON)
    up = a_ref[...].astype(F32) + b_ref[...].astype(F32)
    scaled = up * gain_ref[...]
    grad = inv * scaled - h * (inv * inv * inv) * jnp.mean(scaled * h, axis=-1, keepdims=True)
    out_ref[...] = (rg_ref[...] + grad).astype(BF)


def final(hidden, gain, rg, mine, other):
    length, width = hidden.shape
    blk = 256
    row = pl.BlockSpec((blk, width), lambda i: (i, 0))
    return pl.pallas_call(
        final_body,
        grid=(length // blk,),
        in_specs=[row, whole((1, width)), row, row, row],
        out_specs=row,
        out_shape=jax.ShapeDtypeStruct((length, width), BF),
        compiler_params=params(),
        cost_estimate=cost(20 * length * width, 9 << 20),
        name="final",
    )(hidden, gain, rg, mine, other)


def exchange(values, groups=None):
    return lax.all_to_all(
        values, "expert", split_axis=0, concat_axis=0, tiled=True, axis_index_groups=groups
    )


def after(value, *events):
    return lax.optimization_barrier((value, *events))[0]


def swap(values):
    return lax.ppermute(values, "tensor", [(0, 1), (1, 0)])


def local(
    hidden_in, w_qkv, w_out, gain_in, gain_mid, w_router, w_const, const_vec,
    w_gate, w_up, w_down, prev_logits, routes, doc_ids, span_start, span_len, d_output,
):
    length, width = hidden_in.shape
    experts, share, units = w_gate.shape
    inner = w_qkv.shape[2]
    peers = lax.axis_size("expert")
    copies = peers // experts

    def cross(blocks):
        steps = [b ^ (experts // 2) for b in range(experts)]
        return [
            lax.ppermute(blk, "expert", [(i, i ^ d) for i in range(peers)]) if d else blk
            for blk, d in zip(blocks, steps)
        ]

    def both(blocks):
        return blocks + [swap(blk) for blk in blocks]

    routes_total = w_router.shape[1]

    def fetch(parts):
        stacked = jnp.stack(parts, axis=1).reshape(1, experts, len(parts) * share, -1)
        sent = jnp.broadcast_to(stacked, (copies,) + stacked.shape[1:])
        return sent.reshape(peers, len(parts) * share, -1)

    def rows_first(got, parts):
        got = got.reshape(peers, parts, share, -1)
        if share % 16:
            got = got.transpose(1, 0, 2, 3).reshape(1, parts, width, -1)
        return got

    def peers_first(grads):
        if share % 16:
            grads = grads.reshape(-1, peers, share, units).transpose(1, 0, 2, 3)
        return grads.reshape(peers, -1, units)

    part = units // 2
    first_sent = fetch([w[:, :, :part] for w in (w_gate, w_up, w_down)])
    second_sent = fetch([w[:, :, part:] for w in (w_gate, w_up, w_down)])
    first_trio = rows_first(exchange(first_sent), 3)
    pack = first_trio.shape[0]

    lane = np.arange(128)
    frequency = 10000.0 ** (-jnp.asarray(lane % (HD // 2)).astype(F32) / (HD // 2))
    phase = jnp.arange(length).astype(F32)[:, None] * frequency[None, :]
    cos = jnp.cos(phase)
    sin = jnp.where((lane % HD < HD // 2)[None, :], -jnp.sin(phase), jnp.sin(phase))
    cuts = jnp.sum(doc_ids[None, :] < jnp.arange(1, 4)[:, None], axis=1, dtype=jnp.int32)
    meta = jnp.concatenate(
        [span_start[0], span_start[0] + span_len[0], cuts, jnp.zeros((1,), jnp.int32)]
    )

    place = jnp.stack([lax.axis_index("tensor"), lax.axis_index("expert")]).astype(jnp.int32)
    col = route_call(place, routes.T, experts)

    w3 = w_qkv.transpose(1, 0, 2)
    normed_in, q, k, v = qkv(after(hidden_in, col), gain_in.reshape(1, width), w3, cos, sin)
    context, lse = attend(meta, q, k, v)
    attended = jnp.dot(context, w_out, preferred_element_type=F32)
    joint = jnp.concatenate([w_router.T, w_const.T], axis=0)
    r, n, rows, cols, *blocks = mid(
        hidden_in, attended, swap(attended), gain_mid.reshape(1, width), joint,
        prev_logits.T, routes.T, col, d_output,
    )
    crossed = cross(blocks)
    second_sent = after(second_sent, first_trio, n)
    second_trio = rows_first(exchange(second_sent), 3)
    x, dy, hid, gp, up, partial = ffn_first(both(crossed), first_trio)
    *other_saved, other_out = ffn_second(1, x, dy, partial, second_trio)
    *mine_saved, mine_out = ffn_second(0, x, dy, partial, second_trio)
    back = cross(join(mine_out, swap(other_out), experts))
    grads = learn(after(x, back[0]), dy, [hid, gp, up, *mine_saved, *other_saved], pack)
    parted = exchange(after(peers_first(grads), *back))
    back = both([after(blk, grads) for blk in back])

    output, prev_grad, rg, ag, small = combine(
        back, r, n, rows, cols, gain_mid.reshape(1, width), const_vec, joint, d_output
    )
    args = (meta, q, k, v, context, lse, ag, w_out, cos, sin)
    pairs = inner // 128
    first = attend_back(*args, 0, pairs - 1)
    folded = share % 16 == 0
    if folded:
        early = shared_call(
            place, [ag, normed_in], (0, 1, 1, 1), [context, *first], [], inner, peers
        )
        args = (meta, after(q, early[0]), *args[2:])
    second = attend_back(*args, pairs - 1, 1, 30000)
    normed_grad, gain_part = inward([*first, *second], w3, hidden_in)
    if folded:
        tail = [small, gain_part, swap(gain_part)]
        late = shared_call(place, [normed_in], (0, 0, 0), second, tail, inner, peers)
        rg = after(rg, late[0])
    grad_input = final(
        hidden_in, gain_in.reshape(1, width), rg, normed_grad, swap(normed_grad)
    )
    parted = [parted.reshape(copies, experts, 3, share, units)]
    if not folded:
        gate_grad, up_grad, down_grad = (
            jnp.concatenate([jnp.sum(p[:, :, m].astype(F32), axis=0) for p in parted], axis=2)
            for m in range(3)
        )
        whole_grads = [jnp.concatenate(pieces, axis=1) for pieces in zip(first, second)]
        outer = [tn(normed_in, grad) for grad in whole_grads] + [tn(ag, context)]
        outer = jnp.stack([g.reshape(peers, share, inner) for g in outer], axis=1)
        shared = jnp.sum(exchange(outer.astype(BF)).astype(F32), axis=0)
        gain_part = gain_part[0:1] + swap(gain_part)[0:1]
        small = jnp.concatenate([small[:19], gain_part, small[20:]], axis=0)
        small = jnp.sum(exchange(small.reshape(24, peers, share).transpose(1, 0, 2)), axis=0)
        qkv_grad, wout_grad = shared[0:3], shared[3]
        router_grad, const_grad = small[0:routes_total], small[routes_total : routes_total + 4]
        cvec_grad, mid_gain, in_gain = small[16:18], small[18:19], small[19:20]
    else:

        def hop(values, distance):
            return lax.ppermute(values, "expert", [(i, i ^ distance) for i in range(peers)])

        def fold(keep, send, bit):
            total = keep.astype(F32) + hop(send, bit).astype(F32)
            return total.astype(BF)

        gate_grad, up_grad, down_grad = total_call(*parted)
        size = peers // 4
        early_x = fold(*early, 1)
        late_x = fold(after(late[0], early_x), late[1], 1)
        early_y = fold(after(early_x[:size], grad_input), early_x[size:], 2)
        late_y = fold(after(late_x[:size], early_y), late_x[size:], 2)
        both_y = jnp.concatenate([early_y, late_y], axis=1)
        parts = [after(both_y, down_grad)] + [hop(both_y[j], 4 * j) for j in range(1, size)]
        (qkv_grad, wout_grad, router_grad, const_grad, cvec_grad, mid_gain, in_gain) = gather(
            parts, routes_total, share, inner
        )

    return (
        output,
        grad_input,
        prev_grad.T,
        qkv_grad.transpose(1, 0, 2),
        wout_grad.T,
        in_gain.reshape(share),
        mid_gain.reshape(share),
        router_grad.T,
        const_grad.T,
        cvec_grad,
        gate_grad,
        up_grad,
        down_grad,
    )


def solution(mesh):
    rows = P("expert", None)
    expert_spec = P(None, "expert", "tensor")
    return jax.shard_map(
        local,
        mesh=mesh,
        in_specs=(
            rows, P(None, None, "tensor"), P("tensor", None), P(), P(), P(), P(), P(),
            expert_spec, expert_spec, expert_spec, rows, rows, P("expert"), rows, rows, rows,
        ),
        out_specs=(
            rows, rows, rows, P("expert", None, "tensor"), P("tensor", "expert"),
            P("expert"), P("expert"), rows, rows, P(None, "expert"),
            expert_spec, expert_spec, expert_spec,
        ),
        check_vma=False,
    )
```
